32 devices in a mesh: enc: 8 (over y, x, core), dec: 4 (over z).
Axes of the slice: x: 2, y: 2, z: 4, core: 2. Of those that a mesh axis runs over, the one named last changes fastest.
Arguments:
- queries: bfloat16 [2048, 4096], P('dec', 'enc'), may hold values from -16 to 16
- out_grad: bfloat16 [2048, 4096], P('dec', 'enc'), may hold values from -6 to 6
- memory_keys: bfloat16 [4096, 4096], P('enc'), may hold values from -6 to 6
- memory_values: bfloat16 [4096, 4096], P('enc'), may hold values from -6 to 6
- ref_blocks: int32 [2048, 8], P('dec'), may hold values from 0 to 31, as said below
- ref_counts: int32 [2048], P('dec'), may hold values from 1 to 8
Outputs:
- context: bfloat16 [2048, 4096], P('dec', 'enc')
- query_grad: bfloat16 [2048, 4096], P('dec', 'enc')
- key_grad: bfloat16 [4096, 4096], P('enc', 'dec')
- value_grad: bfloat16 [4096, 4096], P('enc', 'dec')
The draws below stay inside these ranges and needn't reach their ends.
Inputs may be any that keep to these rules, and one draw needn't show every extreme that they name: `ref_blocks`: each row holds 8 different block numbers.
All inputs are finite; a program needn't handle non-finite values.
Results may differ from the reference program's by a relative error of at most 0.0092.
Values may be sent and summed in bfloat16 or wider, within the bound.
A program may use at most 192 MiB of HBM per device.

```python
import jax
import jax.numpy as jnp
from jax import lax

HEADS = 64
DH = 64
D = 4096
BLOCK = 128
REFS = 8
TOK_DEV = 512
CELLS = 4096
BLOCKS = 32
TOKENS = 2048


def sheet_refs(key):
    sub_key = jax.random.fold_in(key, 7)
    random_part = jax.random.randint(sub_key, (TOKENS, BLOCKS), 0, 1024)
    columns = jnp.arange(BLOCKS, dtype=jnp.int32)
    weights = 10 + 20 * columns // BLOCKS
    scores = random_part * weights[None, :] * BLOCKS + columns[None, :]
    return lax.top_k(scores, REFS)[1].astype(jnp.int32)


def sheet_keys(key):
    sub_key = jax.random.fold_in(key, 3)
    base = jnp.clip(jax.random.normal(sub_key, (CELLS, D), jnp.float32), -4.0, 4.0)
    rising = 0.8 + 0.6 * jnp.arange(CELLS, dtype=jnp.float32) / CELLS
    memory = base * rising[:, None]
    return memory


def draw_memory_keys(key, part):
    return sheet_keys(key).astype(jnp.bfloat16)


def draw_queries(key, part):
    sub_key = jax.random.fold_in(key, 5)
    base = 0.125 * jnp.clip(jax.random.normal(sub_key, (TOKENS, D), jnp.float32), -4.0, 4.0)
    return base.astype(jnp.bfloat16)


def draw_ref_blocks(key, part):
    return sheet_refs(key)


def with_ends(values, own_key, low, high):
    longest = values.shape.index(max(values.shape))
    spots = []
    for shift in (0, 1):
        where = [jax.random.randint(jax.random.fold_in(own_key, axis), (), 0, length) for axis, length in enumerate(values.shape)]
        where[longest] = (where[longest] + shift) % values.shape[longest]
        spots.append(tuple(where))
    return values.at[spots[0]].set(low).at[spots[1]].set(high)


def block_levels(own_key, dims, split, low, high):
    def one(dim, parts):
        draws = jax.random.uniform(jax.random.fold_in(jax.random.fold_in(own_key, 6), dim), (parts,), jnp.float32, low / len(split), high / len(split))
        return jnp.repeat(jnp.exp(draws), dims[dim] // parts).reshape((-1,) + (1,) * (len(dims) - dim - 1))

    loudness = one(*split[0])
    for cut in split[1:]:
        loudness = loudness * one(*cut)
    return loudness


def gaussian(own_key, extent, deviation, most, pieces=(), kind=jnp.bfloat16):
    result = jax.random.normal(own_key, extent, jnp.float32) * deviation
    if len(pieces) > 0:
        result = block_levels(own_key, extent, pieces, -0.22, 0.18) * result
    return jnp.clip(result, min=-most, max=most).astype(kind)


def setup_inputs(seed: int = 0) -> dict:
    streams_of = jax.random.split(jax.random.key(seed), 7)
    queries = draw_queries(jax.random.fold_in(streams_of[6], 71), 0)
    out_grad = gaussian(streams_of[1], (TOKENS, D), 1.0, 6.0, ((0, 4), (1, 8)))
    memory_keys = draw_memory_keys(jax.random.fold_in(streams_of[6], 71), 0)
    memory_values = gaussian(streams_of[3], (CELLS, D), 1.0, 6.0, ((0, 8),))
    ref_blocks = draw_ref_blocks(jax.random.fold_in(streams_of[6], 71), 0)
    ref_counts = with_ends(jax.random.randint(streams_of[5], (TOKENS,), 1, REFS + 1), jax.random.fold_in(streams_of[5], 1), 1, REFS).astype(jnp.int32)
    return {"queries": queries, "out_grad": out_grad, "memory_keys": memory_keys, "memory_values": memory_values, "ref_blocks": ref_blocks, "ref_counts": ref_counts}


NEGATIVE = -1e30


def reference(queries, out_grad, memory_keys, memory_values, ref_blocks, ref_counts):
    token_count = queries.shape[0]
    cell_count = memory_keys.shape[0]
    block_count = cell_count // BLOCK
    head_queries = queries.reshape(token_count, HEADS, DH).transpose(1, 0, 2)
    head_grads = out_grad.reshape(token_count, HEADS, DH).transpose(1, 0, 2)
    head_keys = memory_keys.reshape(block_count, BLOCK, HEADS, DH).transpose(2, 0, 1, 3)
    head_values = memory_values.reshape(block_count, BLOCK, HEADS, DH).transpose(2, 0, 1, 3)
    live_slot = jnp.arange(REFS, dtype=jnp.int32)[None, :] < ref_counts[:, None]
    block_rows = TOK_DEV
    row_blocks = token_count // block_rows
    refs_split = ref_blocks.reshape(row_blocks, block_rows, REFS)
    live_split = live_slot.reshape(row_blocks, block_rows, REFS)

    def one_head(carry, head_data):
        query_head, grad_head, key_head, value_head = head_data
        query_split = query_head.reshape(row_blocks, block_rows, DH)
        grad_split = grad_head.reshape(row_blocks, block_rows, DH)

        def one_block(accum, block_data):
            key_acc, value_acc = accum
            query_rows, grad_rows, ref_rows, live_rows = block_data
            query_wide = query_rows.astype(jnp.float32)
            grad_wide = grad_rows.astype(jnp.float32)
            key_sel = key_head[ref_rows].astype(jnp.float32)
            value_sel = value_head[ref_rows].astype(jnp.float32)
            scores = jnp.einsum("td,trcd->trc", query_wide, key_sel)
            scores = jnp.where(live_rows[:, :, None], scores, NEGATIVE)
            row_max = jnp.max(scores, axis=(1, 2), keepdims=True)
            log_total = row_max + jnp.log(jnp.sum(jnp.exp(scores - row_max), axis=(1, 2), keepdims=True))
            soft_weights = jnp.exp(scores - log_total)
            rounded_wide = lax.optimization_barrier(soft_weights.astype(jnp.bfloat16)).astype(jnp.float32)
            attended = jnp.einsum("trc,trcd->td", rounded_wide, value_sel)
            row_term = jnp.sum(grad_wide * attended, axis=1)
            weight_grad = jnp.einsum("td,trcd->trc", grad_wide, value_sel)
            score_grad = (soft_weights * (weight_grad - row_term[:, None, None])).astype(jnp.bfloat16)
            score_wide = lax.optimization_barrier(score_grad).astype(jnp.float32)
            query_term = jnp.einsum("trc,trcd->td", score_wide, key_sel)
            key_terms = jnp.einsum("trc,td->trcd", score_wide, query_wide)
            value_terms = jnp.einsum("trc,td->trcd", rounded_wide, grad_wide)
            key_acc = key_acc.at[ref_rows].add(key_terms)
            value_acc = value_acc.at[ref_rows].add(value_terms)
            return (key_acc, value_acc), (attended, query_term)

        zero_grid = jnp.zeros((block_count, BLOCK, DH), jnp.float32)
        sums, rows_out = lax.scan(one_block, (zero_grid, zero_grid), (query_split, grad_split, refs_split, live_split))
        attended, query_term = rows_out
        key_acc, value_acc = sums
        return carry, (attended.reshape(token_count, DH), query_term.reshape(token_count, DH),
                       key_acc.reshape(cell_count, DH), value_acc.reshape(cell_count, DH))

    unused, outputs = lax.scan(one_head, jnp.zeros((), jnp.float32), (head_queries, head_grads, head_keys, head_values))
    attended, query_term, key_term, value_term = outputs
    context = attended.transpose(1, 0, 2).reshape(token_count, HEADS * DH).astype(jnp.bfloat16)
    query_grad = query_term.transpose(1, 0, 2).reshape(token_count, HEADS * DH).astype(jnp.bfloat16)
    key_grad = key_term.transpose(1, 0, 2).reshape(cell_count, HEADS * DH).astype(jnp.bfloat16)
    value_grad = value_term.transpose(1, 0, 2).reshape(cell_count, HEADS * DH).astype(jnp.bfloat16)
    return (context, query_grad, key_grad, value_grad)
```

```python
import functools

import jax
import jax.numpy as jnp
import numpy as np
from jax import lax
from jax.experimental import pallas as pl
from jax.experimental.pallas import tpu as pltpu
from jax.sharding import PartitionSpec as P

DH = 64
BLOCK = 128
HIDDEN = -1e30
LANES = 128


def nt(a, b):
    return lax.dot_general(a, b, (((1,), (1,)), ((), ())), preferred_element_type=jnp.float32)


def nn(a, b):
    return lax.dot_general(a, b, (((1,), (0,)), ((), ())), preferred_element_type=jnp.float32)


def attention_kernel(
    heads, chunk, k_ref, v_ref, e_ref, q_ref, g_ref, bias_ref,
    ctx_ref, dq_ref, dk_ref, dv_ref,
    kt, vt, s_buf, e_buf, dk_acc, dv_acc,
):
    step = pl.program_id(0)
    cells, width = k_ref.shape
    rows = q_ref.shape[0]
    chunks = cells // chunk

    @pl.when(step == 0)
    def _():
        def prepare(i, _):
            at = pl.ds(pl.multiple_of(i * chunk, chunk), chunk)
            kt[:, at] = k_ref[at, :].T
            vt[:, at] = v_ref[at, :].T
            dk_acc[at, :] = jnp.zeros((chunk, width), jnp.float32)
            dv_acc[at, :] = jnp.zeros((chunk, width), jnp.float32)
            return 0

        lax.fori_loop(0, chunks, prepare, 0)

    lane = lax.broadcasted_iota(jnp.int32, (rows, width), 1)
    own = [(lane >= h * DH) & (lane < (h + 1) * DH) for h in range(heads)]
    q = q_ref[...]
    q_own = [jnp.where(own[h], q, jnp.zeros_like(q)) for h in range(heads)]
    bias = bias_ref[...].astype(jnp.float32)
    blank = jnp.zeros((LANES - bias.shape[0], rows), jnp.float32)
    bias = jnp.concatenate([bias, blank], axis=0).T.astype(jnp.bfloat16)
    q_aug = [jnp.concatenate([q_own[h], bias], axis=1) for h in range(heads)]

    def score_chunk(i, tops):
        at = pl.ds(pl.multiple_of(i * chunk, chunk), chunk)
        left = jnp.concatenate([k_ref[at, :], e_ref[at, :]], axis=1)
        out = []
        for h in range(heads):
            s = nt(left, q_aug[h])
            s_buf[h, at, :] = s
            out.append(jnp.maximum(tops[h], jnp.max(s.reshape(chunk // 8, 8, rows), axis=0)))
        return tuple(out)

    tops = lax.fori_loop(
        0, chunks, score_chunk, tuple(jnp.full((8, rows), -3e38, jnp.float32) for _ in range(heads))
    )
    top = [jnp.max(t, axis=0, keepdims=True) for t in tops]

    def weight_chunk(i, carry):
        at = pl.ds(pl.multiple_of(i * chunk, chunk), chunk)
        totals, outs = carry
        new_totals, new_outs = [], []
        for h in range(heads):
            e = jnp.exp(s_buf[h, at, :] - top[h])
            new_totals.append(totals[h] + jnp.sum(e.reshape(chunk // 8, 8, rows), axis=0))
            e = e.astype(jnp.bfloat16)
            e_buf[h, at, :] = e
            new_outs.append(outs[h] + nn(vt[h * DH : (h + 1) * DH, at], e))
        return tuple(new_totals), tuple(new_outs)

    totals, outs = lax.fori_loop(
        0,
        chunks,
        weight_chunk,
        (
            tuple(jnp.zeros((8, rows), jnp.float32) for _ in range(heads)),
            tuple(jnp.zeros((DH, rows), jnp.float32) for _ in range(heads)),
        ),
    )
    inv = [1.0 / jnp.sum(t, axis=0, keepdims=True) for t in totals]
    stack = jnp.concatenate(
        [outs[h] * inv[h] for h in range(heads)]
        + [jnp.broadcast_to(inv[h], (DH, rows)) for h in range(heads)],
        axis=0,
    ).T
    attended = stack[:, :width]
    ctx_ref[...] = attended.astype(ctx_ref.dtype)
    g_scaled = (g_ref[...].astype(jnp.float32) * stack[:, width:]).astype(jnp.bfloat16)
    product = g_scaled.astype(jnp.float32) * attended
    lane_aug = lax.broadcasted_iota(jnp.int32, (rows, LANES), 1)
    g_own, g_aug = [], []
    for h in range(heads):
        term = -jnp.sum(jnp.where(own[h], product, 0.0), axis=1, keepdims=True)
        high = term.astype(jnp.bfloat16).astype(jnp.float32)
        low = term - high
        extra = jnp.where(
            lane_aug == LANES - 1, high, jnp.where(lane_aug == LANES - 2, low, 0.0)
        ).astype(jnp.bfloat16)
        g_own.append(jnp.where(own[h], g_scaled, jnp.zeros_like(g_scaled)))
        g_aug.append(jnp.concatenate([g_own[h], extra], axis=1))
    q_all = jnp.concatenate(q_own, axis=0)
    g_all = jnp.concatenate(g_own, axis=0)

    def grad_chunk(i, dqs):
        at = pl.ds(pl.multiple_of(i * chunk, chunk), chunk)
        left = jnp.concatenate([v_ref[at, :], e_ref[at, :]], axis=1)
        new_dqs, ds_all, e_all = [], [], []
        for h in range(heads):
            e = e_buf[h, at, :]
            ds = (e.astype(jnp.float32) * nt(left, g_aug[h])).astype(jnp.bfloat16)
            new_dqs.append(dqs[h] + nn(kt[h * DH : (h + 1) * DH, at], ds))
            ds_all.append(ds)
            e_all.append(e)
        dk_acc[at, :] += nn(jnp.concatenate(ds_all, axis=1), q_all)
        dv_acc[at, :] += nn(jnp.concatenate(e_all, axis=1), g_all)
        return tuple(new_dqs)

    dqs = lax.fori_loop(
        0, chunks, grad_chunk, tuple(jnp.zeros((DH, rows), jnp.float32) for _ in range(heads))
    )
    dq_ref[...] = jnp.concatenate(dqs, axis=0).T.astype(dq_ref.dtype)

    @pl.when(step == pl.num_programs(0) - 1)
    def _():
        dk_ref[...] = dk_acc[...].astype(dk_ref.dtype)
        dv_ref[...] = dv_acc[...].astype(dv_ref.dtype)


def cell_marks(cells):
    block_ids = lax.broadcasted_iota(jnp.int32, (cells, LANES), 0) // BLOCK
    lane = lax.broadcasted_iota(jnp.int32, (cells, LANES), 1)
    return ((block_ids == lane) | (lane >= LANES - 2)).astype(jnp.bfloat16)


def attention(q, g, k, v, bias, grad_type=jnp.bfloat16, rows=512, chunk=2048):
    tokens, width = q.shape
    cells = k.shape[0]
    heads = width // DH
    chunk = min(chunk, cells)
    whole = lambda i: (0, 0)
    part = lambda i: (i, 0)
    cell_spec = pl.BlockSpec((cells, width), whole)
    token_spec = pl.BlockSpec((rows, width), part)
    bf = jnp.bfloat16
    return pl.pallas_call(
        functools.partial(attention_kernel, heads, chunk),
        grid=(tokens // rows,),
        out_shape=(
            jax.ShapeDtypeStruct((tokens, width), bf),
            jax.ShapeDtypeStruct((tokens, width), bf),
            jax.ShapeDtypeStruct((cells, width), grad_type),
            jax.ShapeDtypeStruct((cells, width), grad_type),
        ),
        in_specs=[
            cell_spec,
            cell_spec,
            pl.BlockSpec((cells, LANES), whole),
            token_spec,
            token_spec,
            pl.BlockSpec((bias.shape[0], rows), lambda i: (0, i)),
        ],
        out_specs=(token_spec, token_spec, cell_spec, cell_spec),
        scratch_shapes=[
            pltpu.VMEM((width, cells), bf),
            pltpu.VMEM((width, cells), bf),
            pltpu.VMEM((heads, cells, rows), jnp.float32),
            pltpu.VMEM((heads, cells, rows), bf),
            pltpu.VMEM((cells, width), jnp.float32),
            pltpu.VMEM((cells, width), jnp.float32),
        ],
        compiler_params=pltpu.CompilerParams(vmem_limit_bytes=60 * 1024 * 1024),
        name="attention",
    )(k, v, cell_marks(cells), q, g, bias)


def hidden_blocks(ref_blocks, ref_counts, blocks):
    slot_ids = jnp.arange(ref_blocks.shape[1], dtype=jnp.int32)
    live = slot_ids[None, :] < ref_counts[:, None]
    wanted = jnp.where(live, ref_blocks, -1).T
    seen = jnp.any(wanted[:, None, :] == jnp.arange(blocks, dtype=jnp.int32)[:, None], axis=0)
    return jnp.where(seen, 0.0, HIDDEN).astype(jnp.bfloat16)


def greet_all():
    barrier = pltpu.get_barrier_semaphore()
    enc, dec = lax.axis_size("enc"), lax.axis_size("dec")
    me = lax.axis_index("enc") * dec + lax.axis_index("dec")

    def greet(d, _):
        other = lax.rem(me + d, enc * dec)
        pl.semaphore_signal(
            barrier, inc=1, device_id=(other // dec, lax.rem(other, dec)),
            device_id_type=pl.DeviceIdType.MESH,
        )
        return 0

    lax.fori_loop(1, enc * dec, greet, 0)
    pl.semaphore_wait(barrier, enc * dec - 1)


def remote(src, dst, send, recv, target):
    return pltpu.make_async_remote_copy(
        src_ref=src, dst_ref=dst, send_sem=send, recv_sem=recv,
        device_id=target, device_id_type=pl.DeviceIdType.MESH,
    )


def lanes(ref, index, width):
    return ref.at[:, pl.ds(pl.multiple_of(index * width, width), width)]


def flip(x, d):
    parts = [lax.rem(lax.div(x, b) + lax.div(jnp.int32(d), b), 2) * b for b in (1, 2, 4)]
    return parts[0] + parts[1] + parts[2]


def fused_kernel(
    q, g, k, v, bias, ctx_o, dq_o, dk_o, dv_o,
    q_mid, g_mid, q_in, g_in, k_in, v_in, bias_in, kl, vl, kt, vt, qt, gt,
    s_buf, e_buf, m_buf, m_run, o_acc, inv_buf, term_buf, dq_acc, dk_acc, dv_acc,
    cell_out, ctx_out, dq_out,
    mid_send, mid_recv, tok_send, tok_recv, bias_send, bias_recv, cell_send, cell_recv,
    grad_send, grad_recv, back_send, back_recv, local,
):
    enc, dec = lax.axis_size("enc"), lax.axis_size("dec")
    per = enc // dec
    e, z = lax.axis_index("enc"), lax.axis_index("dec")
    home, core = lax.div(e, per), lax.rem(e, per)
    chunk, width = k_in.shape[1], k_in.shape[2]
    tok = q_in.shape[1]
    heads = width // DH
    piece = chunk // 2
    bf, f32 = jnp.bfloat16, jnp.float32
    near = lambda x: lax.rem(x, per) * dec + lax.div(x, per)
    slot = lambda x: z * enc + near(x)
    mine = home == z
    tokens = ((q, q_mid, q_in), (g, g_mid, g_in))
    greet_all()

    def plane_copy(n, d):
        src, mid, dst = tokens[n]
        i = lax.rem(home + d, dec)
        return remote(
            lanes(src, i, width), mid.at[home], mid_send.at[n, d], mid_recv.at[n, d],
            (per * i + core, z),
        )

    def pass_on(n, d, act):
        src, mid, dst = tokens[n]
        j = lax.rem(home - d + dec, dec)
        piece = lanes(src, home, width) if d == 0 else mid.at[j]
        here = dst.at[z]

        @pl.when(j == z)
        def _():
            act(pltpu.make_async_copy(piece, here, local.at[n]), True)

        @pl.when(j != z)
        def _():
            act(remote(piece, here, tok_send.at[n, d], tok_recv.at[n, z], (e, j)), False)

    def begin(copy, stays):
        copy.start()

    def finish(copy, stays):
        if not stays:
            copy.wait_send()

    def token_start(n):
        for d in range(1, dec):
            plane_copy(n, d).start()
        pass_on(n, 0, begin)

    def token_turn(n):
        src, mid, dst = tokens[n]
        for d in range(1, dec):
            j = lax.rem(home - d + dec, dec)
            remote(
                lanes(src, 0, width), mid.at[j], mid_send.at[n, d], mid_recv.at[n, d],
                (per * j + core, z),
            ).wait_recv()
            pass_on(n, d, begin)

    def token_ready(n, t):
        src, mid, dst = tokens[n]

        @pl.when(t == z)
        def _():
            pltpu.make_async_copy(lanes(src, home, width), dst.at[z], local.at[n]).wait()

        @pl.when(t != z)
        def _():
            remote(
                lanes(src, 0, width), dst.at[t], tok_send.at[n, 0], tok_recv.at[n, t], (e, t)
            ).wait_recv()

    def token_sent(n):
        for d in range(1, dec):
            plane_copy(n, d).wait_send()
        for d in range(dec):
            pass_on(n, d, finish)

    def bias_copy(i):
        return remote(
            bias, bias_in.at[z], bias_send.at[i], bias_recv.at[z], (e, lax.rem(z + i, dec))
        )

    bias_local = pltpu.make_async_copy(bias, bias_in.at[z], local.at[2])

    def bias_ready(t):
        pl.when(t == z)(lambda: bias_local.wait())

        @pl.when(t != z)
        def _():
            remote(bias, bias_in.at[t], bias_send.at[0], bias_recv.at[t], (e, z)).wait_recv()

    def cell_copy(n, src, dst, d):
        other = flip(e, d)
        return remote(
            lanes(src, slot(other), width), dst.at[d], cell_send.at[n, d], cell_recv.at[n, d],
            (other, z),
        )

    def cell_local(n, src, dst):
        return pltpu.make_async_copy(lanes(src, slot(e), width), dst.at[0], local.at[3 + n])

    def grad_copy(n, dst, d):
        other = flip(e, d)
        return remote(
            cell_out.at[n, d], lanes(dst, near(e), width), grad_send.at[n, d],
            grad_recv.at[n, d], (other, z),
        )

    def grad_wait(n, dst, d):
        other = flip(e, d)
        return remote(
            cell_out.at[n, d], lanes(dst, near(other), width), grad_send.at[n, d],
            grad_recv.at[n, d], (other, z),
        )

    def grad_local(n, dst):
        return pltpu.make_async_copy(
            cell_out.at[n, 0], lanes(dst, near(e), width), local.at[5 + n]
        )

    def back_copy(n, src, dst, t):
        return remote(
            src.at[t], lanes(dst, home, width), back_send.at[n, t], back_recv.at[n, home],
            (per * z + core, t),
        )

    def back_local(n, src, dst):
        return pltpu.make_async_copy(src.at[z], lanes(dst, home, width), local.at[7 + n])

    def back_start(n, src, dst, t):
        here = mine & (t == z)
        pl.when(here)(lambda: back_local(n, src, dst).start())
        pl.when(jnp.logical_not(here))(lambda: back_copy(n, src, dst, t).start())

    def back_finish(n, src, dst):
        for t in range(dec):
            here = mine & (t == z)
            pl.when(here)(lambda: back_local(n, src, dst).wait())
            pl.when(jnp.logical_not(here))(lambda: back_copy(n, src, dst, t).wait_send())
        for i in range(dec):

            @pl.when(jnp.logical_not(mine & (home == i)))
            def _():
                remote(
                    src.at[0], lanes(dst, i, width), back_send.at[n, 0], back_recv.at[n, i],
                    (e, z),
                ).wait_recv()

    token_start(0)
    for i in range(1, dec):
        bias_copy(i).start()
    bias_local.start()
    for n, src, dst in ((0, k, k_in), (1, v, v_in)):
        cell_local(n, src, dst).start()
        cell_copy(n, src, dst, 1).start()
    for d in range(2, enc):
        cell_copy(0, k, k_in, d).start()
        cell_copy(1, v, v_in, d).start()
        if d == 3:
            token_start(1)

    m_run[...] = jnp.full(m_run.shape, -3e38, f32)
    o_acc[...] = jnp.zeros(o_acc.shape, f32)
    dq_acc[...] = jnp.zeros(dq_acc.shape, f32)

    def prepare_tokens(t):
        token_ready(0, t)
        bias_ready(t)
        turned = q_in[t].T
        hidden = bias_in[t]
        blank = jnp.zeros((DH - hidden.shape[0], tok), bf)
        qt[t, 0] = jnp.concatenate([turned[:DH], hidden, blank], axis=0)
        qt[t, 1] = jnp.concatenate([hidden, blank, turned[DH:]], axis=0)

    def prepare_chunk(d):
        kc, vc = k_in[d], v_in[d]
        lane = lax.broadcasted_iota(jnp.int32, (chunk, width), 1)
        block = flip(e, d) * (chunk // BLOCK) + lax.broadcasted_iota(
            jnp.int32, (chunk, width), 0
        ) // BLOCK
        ones = jnp.where(
            lax.broadcasted_iota(jnp.int32, (16, chunk), 0) == 0, 1.0, 0.0
        ).astype(bf)
        turned = vc.T
        for h in range(heads):
            own = (lane >= h * DH) & (lane < (h + 1) * DH)
            spare = lane - (heads - 1 - h) * DH
            kl[d, h] = jnp.where(own, kc, jnp.where(spare == block, 1.0, 0.0).astype(bf))
            pair = (spare == 0) | (spare == 1)
            vl[d, h] = jnp.where(own, vc, jnp.where(pair, 1.0, 0.0).astype(bf))
            vt[d, h] = jnp.concatenate([turned[h * DH : (h + 1) * DH], ones], axis=0)
        kt[d] = kc.T

    def forward(d, t):
        for h in range(heads):
            top8 = jnp.full((8, tok), -3e38, f32)
            for i in range(2):
                s = nn(kl[d, h, i * piece : (i + 1) * piece, :], qt[t, h])
                s_buf[h, i * piece : (i + 1) * piece, :] = s
                top8 = jnp.maximum(top8, jnp.max(s.reshape(piece // 8, 8, tok), axis=0))
            top = jnp.max(top8, axis=0, keepdims=True)
            out = None
            for i in range(2):
                w = jnp.exp(s_buf[h, i * piece : (i + 1) * piece, :] - top).astype(bf)
                e_buf[d, t, h, i * piece : (i + 1) * piece, :] = w
                o = nn(vt[d, h, :, i * piece : (i + 1) * piece], w)
                out = o if out is None else out + o
            before = m_run[t, h, 0:1, :]
            now = jnp.maximum(before, top)
            o_acc[t, h] = o_acc[t, h] * jnp.exp(before - now) + out * jnp.exp(top - now)
            m_run[t, h] = jnp.broadcast_to(now, (8, tok))
            m_buf[d, t, h] = jnp.broadcast_to(top, (8, tok))

    def finish_tokens(t):
        token_ready(1, t)
        turned = g_in[t].T
        gt[t] = turned
        parts = []
        for h in range(heads):
            inv = 1.0 / o_acc[t, h, DH : DH + 1, :]
            part = o_acc[t, h, :DH, :] * inv
            parts.append(part)
            term = jnp.sum(turned[h * DH : (h + 1) * DH].astype(f32) * part, axis=0, keepdims=True)
            inv_buf[t, h] = jnp.broadcast_to(inv, (8, tok))
            term_buf[t, h] = jnp.broadcast_to(-term, (8, tok))
        ctx_out[t] = jnp.concatenate(parts, axis=0).T.astype(bf)
        back_start(0, ctx_out, ctx_o, t)

    def backward(d, t, at):
        lane = lax.broadcasted_iota(jnp.int32, (tok, width), 1)
        own = [(lane >= h * DH) & (lane < (h + 1) * DH) for h in range(heads)]
        row = lax.broadcasted_iota(jnp.int32, (DH, tok), 0)
        scaled, right = [], []
        for h in range(heads):
            factor = jnp.exp(m_buf[d, t, h, 0:1, :] - m_run[t, h, 0:1, :]) * inv_buf[t, h, 0:1, :]
            gs = (gt[t, h * DH : (h + 1) * DH, :].astype(f32) * factor).astype(bf)
            term = term_buf[t, h, 0:1, :] * factor
            high = term.astype(bf).astype(f32)
            extra = jnp.where(row == 0, high, jnp.where(row == 1, term - high, 0.0)).astype(bf)
            scaled.append(gs)
            right.append(jnp.concatenate([gs, extra] if h == 0 else [extra, gs], axis=0))
        g_rows = jnp.concatenate(scaled, axis=0).T
        q_rows = q_in[t]
        g_all = jnp.concatenate([jnp.where(o, g_rows, jnp.zeros_like(g_rows)) for o in own], axis=0)
        q_all = jnp.concatenate([jnp.where(o, q_rows, jnp.zeros_like(q_rows)) for o in own], axis=0)
        dq = [None] * heads
        for i in range(2):
            part = slice(i * piece, (i + 1) * piece)
            ds_all, e_all = [], []
            for h in range(heads):
                w = e_buf[d, t, h, part, :]
                ds = (w.astype(f32) * nn(vl[d, h, part, :], right[h])).astype(bf)
                term = nn(kt[d, h * DH : (h + 1) * DH, part], ds)
                dq[h] = term if dq[h] is None else dq[h] + term
                ds_all.append(ds)
                e_all.append(w)
            dk_acc[at, part, :] += nn(jnp.concatenate(ds_all, axis=1), q_all)
            dv_acc[at, part, :] += nn(jnp.concatenate(e_all, axis=1), g_all)
        dq_acc[t] += jnp.concatenate(dq, axis=0)

    def each(count, step):
        lax.fori_loop(0, count, lambda i, _: (step(i), 0)[1], 0)

    cell_local(0, k, k_in).wait()
    cell_local(1, v, v_in).wait()
    prepare_chunk(0)
    token_turn(0)
    cell_copy(0, k, k_in, 1).wait_recv()
    cell_copy(1, v, v_in, 1).wait_recv()
    prepare_chunk(1)

    def first_tokens(i):
        t = flip(z, i)
        pl.when(i == 1)(lambda: token_turn(1))
        prepare_tokens(t)
        each(2, lambda d: forward(d, t))

    each(dec, first_tokens)

    def next_chunk(n):
        d = n + 2
        cell_copy(0, k, k_in, d).wait_recv()
        cell_copy(1, v, v_in, d).wait_recv()
        prepare_chunk(d)
        each(dec, lambda t: forward(d, t))

    each(enc - 2, next_chunk)
    each(dec, lambda i: finish_tokens(flip(z, dec - 1 - i)))

    def clear(at):
        dk_acc[at] = jnp.zeros((chunk, width), f32)
        dv_acc[at] = jnp.zeros((chunk, width), f32)

    def far_chunk(n):
        d = enc - 2 + lax.rem(n, 2) - 2 * lax.div(n, 2)
        clear(0)
        each(dec, lambda t: backward(d, t, 0))
        cell_out[0, d] = dk_acc[0].astype(bf)
        cell_out[1, d] = dv_acc[0].astype(bf)
        grad_copy(0, dk_o, d).start()
        grad_copy(1, dv_o, d).start()

    each(enc - 2, far_chunk)
    clear(0)
    clear(1)

    def last_tokens(i):
        t = flip(z, dec - 1 - i)
        each(2, lambda d: backward(d, t, d))
        dq_out[t] = dq_acc[t].T.astype(bf)
        back_start(1, dq_out, dq_o, t)

    each(dec, last_tokens)
    for d in range(2):
        cell_out[0, d] = dk_acc[d].astype(bf)
        cell_out[1, d] = dv_acc[d].astype(bf)
    for n, dst in ((0, dk_o), (1, dv_o)):
        grad_copy(n, dst, 1).start()
        grad_local(n, dst).start()

    token_sent(0)
    token_sent(1)
    for i in range(1, dec):
        bias_copy(i).wait_send()
    for d in range(1, enc):
        cell_copy(0, k, k_in, d).wait_send()
        cell_copy(1, v, v_in, d).wait_send()
    for n, dst in ((0, dk_o), (1, dv_o)):
        for d in range(1, enc):
            grad_copy(n, dst, d).wait_send()
            grad_wait(n, dst, d).wait_recv()
        grad_local(n, dst).wait()
    back_finish(0, ctx_out, ctx_o)
    back_finish(1, dq_out, dq_o)


def fused(q, g, k, v, bias):
    enc, dec = lax.axis_size("enc"), lax.axis_size("dec")
    width = k.shape[1] // (enc * dec)
    heads = width // DH
    tok, chunk = q.shape[0], k.shape[0]
    bf, f32 = jnp.bfloat16, jnp.float32
    dma = pltpu.SemaphoreType.DMA
    vmem = pltpu.VMEM
    token_out = jax.ShapeDtypeStruct((tok, dec * width), bf)
    cell_out = jax.ShapeDtypeStruct((chunk, enc * width), bf)
    return pl.pallas_call(
        fused_kernel,
        out_shape=(token_out, token_out, cell_out, cell_out),
        in_specs=[pl.BlockSpec(memory_space=pl.ANY)] * 5,
        out_specs=[pl.BlockSpec(memory_space=pl.ANY)] * 4,
        scratch_shapes=[
            vmem((dec, tok, width), bf), vmem((dec, tok, width), bf),
            vmem((dec, tok, width), bf), vmem((dec, tok, width), bf),
            vmem((enc, chunk, width), bf), vmem((enc, chunk, width), bf),
            vmem((dec, bias.shape[0], tok), bf),
            vmem((enc, heads, chunk, width), bf), vmem((enc, heads, chunk, width), bf),
            vmem((enc, width, chunk), bf), vmem((enc, heads, DH + 16, chunk), bf),
            vmem((dec, heads, width, tok), bf), vmem((dec, width, tok), bf),
            vmem((heads, chunk, tok), f32), vmem((enc, dec, heads, chunk, tok), bf),
            vmem((enc, dec, heads, 8, tok), f32), vmem((dec, heads, 8, tok), f32),
            vmem((dec, heads, DH + 16, tok), f32),
            vmem((dec, heads, 8, tok), f32), vmem((dec, heads, 8, tok), f32),
            vmem((dec, width, tok), f32),
            vmem((2, chunk, width), f32), vmem((2, chunk, width), f32),
            vmem((2, enc, chunk, width), bf), vmem((dec, tok, width), bf),
            vmem((dec, tok, width), bf),
            dma((2, dec)), dma((2, dec)), dma((2, dec)), dma((2, dec)), dma((dec,)), dma((dec,)),
            dma((2, enc)), dma((2, enc)), dma((2, enc)), dma((2, enc)),
            dma((2, dec)), dma((2, dec)), dma((9,)),
        ],
        compiler_params=pltpu.CompilerParams(
            collective_id=0, has_side_effects=True, vmem_limit_bytes=60 * 1024 * 1024
        ),
        name="fused",
    )(q, g, k, v, bias)


def shared_head(q, g, k, v, bias, per, dec):
    share = DH // q.shape[1]
    mates = [
        [per * (j + i) + c for i in range(share)] for c in range(per) for j in range(0, dec, share)
    ]
    place = lax.rem(lax.axis_index("enc") // per, share)
    rows = q.shape[0] // share

    def to_head(x):
        return lax.all_to_all(x, "enc", 0, 1, axis_index_groups=mates, tiled=True)

    def from_head(x):
        return lax.all_to_all(x, "enc", 1, 0, axis_index_groups=mates, tiled=True)

    def widen(x):
        return lax.all_gather(x, "enc", axis=1, axis_index_groups=mates, tiled=True)

    def add_up(x):
        total = lax.psum_scatter(
            x, "enc", scatter_dimension=1, axis_index_groups=mates, tiled=True
        )
        return total.astype(jnp.bfloat16)

    bias = lax.dynamic_slice_in_dim(bias, place * rows, rows, 1)
    ctx, dq, dk, dv = attention(to_head(q), to_head(g), widen(k), widen(v), bias, jnp.float32)
    return from_head(ctx), from_head(dq), add_up(dk), add_up(dv)


def body(queries, out_grad, memory_keys, memory_values, ref_blocks, ref_counts):
    enc, dec = lax.axis_size("enc"), lax.axis_size("dec")
    per = enc // dec
    tok, tok_width = queries.shape
    own_cells, full = memory_keys.shape
    width = full // (enc * dec)
    groups = [[per * k + c for k in range(dec)] for c in range(per)]

    def token_in(x):
        x = x.reshape(tok, dec, width).transpose(1, 0, 2)
        x = lax.all_to_all(x, "enc", 0, 0, axis_index_groups=groups)
        return lax.all_to_all(x, "dec", 0, 0).reshape(dec * tok, width)

    def token_out(x):
        x = lax.all_to_all(x.reshape(dec, tok, width), "dec", 0, 0)
        x = lax.all_to_all(x, "enc", 0, 0, axis_index_groups=groups)
        return x.transpose(1, 0, 2).reshape(tok, tok_width)

    def cell_in(x):
        x = lax.dynamic_slice_in_dim(x, lax.axis_index("dec") * (full // dec), full // dec, 1)
        x = x.reshape(own_cells, per, dec, width).transpose(2, 1, 0, 3)
        x = lax.all_to_all(x.reshape(enc, own_cells, width), "enc", 0, 0)
        return x.reshape(enc * own_cells, width)

    def cell_out(x):
        x = lax.all_to_all(x.reshape(enc, own_cells, width), "enc", 0, 0)
        x = x.reshape(dec, per, own_cells, width).transpose(2, 1, 0, 3)
        return x.reshape(own_cells, full // dec)

    bias = hidden_blocks(ref_blocks, ref_counts, enc * own_cells // BLOCK)
    small = enc * own_cells // BLOCK <= DH
    if width == LANES and enc == 8 and dec == 4 and small:
        return fused(queries, out_grad, memory_keys, memory_values, bias)
    bias = lax.all_gather(bias, "dec", axis=1, tiled=True)
    q, g, k, v = token_in(queries), token_in(out_grad), cell_in(memory_keys), cell_in(memory_values)
    if width >= DH:
        ctx, dq, dk, dv = attention(q, g, k, v, bias)
    else:
        ctx, dq, dk, dv = shared_head(q, g, k, v, bias, per, dec)
    return token_out(ctx), token_out(dq), cell_out(dk), cell_out(dv)


def solution(mesh):
    in_specs = (
        P("dec", "enc"),
        P("dec", "enc"),
        P("enc", None),
        P("enc", None),
        P("dec", None),
        P("dec"),
    )
    out_specs = (P("dec", "enc"), P("dec", "enc"), P("enc", "dec"), P("enc", "dec"))
    return jax.shard_map(body, mesh=mesh, in_specs=in_specs, out_specs=out_specs, check_vma=False)
```

```python
import functools

import jax
import jax.numpy as jnp
import numpy as np
from jax import lax
from jax.experimental import pallas as pl
from jax.experimental.pallas import tpu as pltpu
from jax.sharding import PartitionSpec as P

DH = 64
BLOCK = 128
HIDDEN = -1e30
LANES = 128


def nt(a, b):
    return lax.dot_general(a, b, (((1,), (1,)), ((), ())), preferred_element_type=jnp.float32)


def nn(a, b):
    return lax.dot_general(a, b, (((1,), (0,)), ((), ())), preferred_element_type=jnp.float32)


def attention_kernel(
    heads, chunk, k_ref, v_ref, e_ref, q_ref, g_ref, bias_ref,
    ctx_ref, dq_ref, dk_ref, dv_ref,
    kt, vt, s_buf, e_buf, dk_acc, dv_acc,
):
    step = pl.program_id(0)
    cells, width = k_ref.shape
    rows = q_ref.shape[0]
    chunks = cells // chunk

    @pl.when(step == 0)
    def _():
        def prepare(i, _):
            at = pl.ds(pl.multiple_of(i * chunk, chunk), chunk)
            kt[:, at] = k_ref[at, :].T
            vt[:, at] = v_ref[at, :].T
            dk_acc[at, :] = jnp.zeros((chunk, width), jnp.float32)
            dv_acc[at, :] = jnp.zeros((chunk, width), jnp.float32)
            return 0

        lax.fori_loop(0, chunks, prepare, 0)

    lane = lax.broadcasted_iota(jnp.int32, (rows, width), 1)
    own = [(lane >= h * DH) & (lane < (h + 1) * DH) for h in range(heads)]
    q = q_ref[...]
    q_own = [jnp.where(own[h], q, jnp.zeros_like(q)) for h in range(heads)]
    bias = bias_ref[...].astype(jnp.float32)
    blank = jnp.zeros((LANES - bias.shape[0], rows), jnp.float32)
    bias = jnp.concatenate([bias, blank], axis=0).T.astype(jnp.bfloat16)
    q_aug = [jnp.concatenate([q_own[h], bias], axis=1) for h in range(heads)]

    def score_chunk(i, tops):
        at = pl.ds(pl.multiple_of(i * chunk, chunk), chunk)
        left = jnp.concatenate([k_ref[at, :], e_ref[at, :]], axis=1)
        out = []
        for h in range(heads):
            s = nt(left, q_aug[h])
            s_buf[h, at, :] = s
            out.append(jnp.maximum(tops[h], jnp.max(s.reshape(chunk // 8, 8, rows), axis=0)))
        return tuple(out)

    tops = lax.fori_loop(
        0, chunks, score_chunk, tuple(jnp.full((8, rows), -3e38, jnp.float32) for _ in range(heads))
    )
    top = [jnp.max(t, axis=0, keepdims=True) for t in tops]

    def weight_chunk(i, carry):
        at = pl.ds(pl.multiple_of(i * chunk, chunk), chunk)
        totals, outs = carry
        new_totals, new_outs = [], []
        for h in range(heads):
            e = jnp.exp(s_buf[h, at, :] - top[h])
            new_totals.append(totals[h] + jnp.sum(e.reshape(chunk // 8, 8, rows), axis=0))
            e = e.astype(jnp.bfloat16)
            e_buf[h, at, :] = e
            new_outs.append(outs[h] + nn(vt[h * DH : (h + 1) * DH, at], e))
        return tuple(new_totals), tuple(new_outs)

    totals, outs = lax.fori_loop(
        0,
        chunks,
        weight_chunk,
        (
            tuple(jnp.zeros((8, rows), jnp.float32) for _ in range(heads)),
            tuple(jnp.zeros((DH, rows), jnp.float32) for _ in range(heads)),
        ),
    )
    inv = [1.0 / jnp.sum(t, axis=0, keepdims=True) for t in totals]
    stack = jnp.concatenate(
        [outs[h] * inv[h] for h in range(heads)]
        + [jnp.broadcast_to(inv[h], (DH, rows)) for h in range(heads)],
        axis=0,
    ).T
    attended = stack[:, :width]
    ctx_ref[...] = attended.astype(ctx_ref.dtype)
    g_scaled = (g_ref[...].astype(jnp.float32) * stack[:, width:]).astype(jnp.bfloat16)
    product = g_scaled.astype(jnp.float32) * attended
    lane_aug = lax.broadcasted_iota(jnp.int32, (rows, LANES), 1)
    g_own, g_aug = [], []
    for h in range(heads):
        term = -jnp.sum(jnp.where(own[h], product, 0.0), axis=1, keepdims=True)
        high = term.astype(jnp.bfloat16).astype(jnp.float32)
        low = term - high
        extra = jnp.where(
            lane_aug == LANES - 1, high, jnp.where(lane_aug == LANES - 2, low, 0.0)
        ).astype(jnp.bfloat16)
        g_own.append(jnp.where(own[h], g_scaled, jnp.zeros_like(g_scaled)))
        g_aug.append(jnp.concatenate([g_own[h], extra], axis=1))
    q_all = jnp.concatenate(q_own, axis=0)
    g_all = jnp.concatenate(g_own, axis=0)

    def grad_chunk(i, dqs):
        at = pl.ds(pl.multiple_of(i * chunk, chunk), chunk)
        left = jnp.concatenate([v_ref[at, :], e_ref[at, :]], axis=1)
        new_dqs, ds_all, e_all = [], [], []
        for h in range(heads):
            e = e_buf[h, at, :]
            ds = (e.astype(jnp.float32) * nt(left, g_aug[h])).astype(jnp.bfloat16)
            new_dqs.append(dqs[h] + nn(kt[h * DH : (h + 1) * DH, at], ds))
            ds_all.append(ds)
            e_all.append(e)
        dk_acc[at, :] += nn(jnp.concatenate(ds_all, axis=1), q_all)
        dv_acc[at, :] += nn(jnp.concatenate(e_all, axis=1), g_all)
        return tuple(new_dqs)

    dqs = lax.fori_loop(
        0, chunks, grad_chunk, tuple(jnp.zeros((DH, rows), jnp.float32) for _ in range(heads))
    )
    dq_ref[...] = jnp.concatenate(dqs, axis=0).T.astype(dq_ref.dtype)

    @pl.when(step == pl.num_programs(0) - 1)
    def _():
        dk_ref[...] = dk_acc[...].astype(dk_ref.dtype)
        dv_ref[...] = dv_acc[...].astype(dv_ref.dtype)


def cell_marks(cells):
    block_ids = lax.broadcasted_iota(jnp.int32, (cells, LANES), 0) // BLOCK
    lane = lax.broadcasted_iota(jnp.int32, (cells, LANES), 1)
    return ((block_ids == lane) | (lane >= LANES - 2)).astype(jnp.bfloat16)


def attention(q, g, k, v, bias, grad_type=jnp.bfloat16, rows=512, chunk=2048):
    tokens, width = q.shape
    cells = k.shape[0]
    heads = width // DH
    chunk = min(chunk, cells)
    whole = lambda i: (0, 0)
    part = lambda i: (i, 0)
    cell_spec = pl.BlockSpec((cells, width), whole)
    token_spec = pl.BlockSpec((rows, width), part)
    bf = jnp.bfloat16
    return pl.pallas_call(
        functools.partial(attention_kernel, heads, chunk),
        grid=(tokens // rows,),
        out_shape=(
            jax.ShapeDtypeStruct((tokens, width), bf),
            jax.ShapeDtypeStruct((tokens, width), bf),
            jax.ShapeDtypeStruct((cells, width), grad_type),
            jax.ShapeDtypeStruct((cells, width), grad_type),
        ),
        in_specs=[
            cell_spec,
            cell_spec,
            pl.BlockSpec((cells, LANES), whole),
            token_spec,
            token_spec,
            pl.BlockSpec((bias.shape[0], rows), lambda i: (0, i)),
        ],
        out_specs=(token_spec, token_spec, cell_spec, cell_spec),
        scratch_shapes=[
            pltpu.VMEM((width, cells), bf),
            pltpu.VMEM((width, cells), bf),
            pltpu.VMEM((heads, cells, rows), jnp.float32),
            pltpu.VMEM((heads, cells, rows), bf),
            pltpu.VMEM((cells, width), jnp.float32),
            pltpu.VMEM((cells, width), jnp.float32),
        ],
        compiler_params=pltpu.CompilerParams(vmem_limit_bytes=60 * 1024 * 1024),
        name="attention",
    )(k, v, cell_marks(cells), q, g, bias)


def hidden_blocks(ref_blocks, ref_counts, blocks):
    slot_ids = jnp.arange(ref_blocks.shape[1], dtype=jnp.int32)
    live = slot_ids[None, :] < ref_counts[:, None]
    wanted = jnp.where(live, ref_blocks, -1).T
    seen = jnp.any(wanted[:, None, :] == jnp.arange(blocks, dtype=jnp.int32)[:, None], axis=0)
    return jnp.where(seen, 0.0, HIDDEN).astype(jnp.bfloat16)


def greet_all():
    barrier = pltpu.get_barrier_semaphore()
    enc, dec = lax.axis_size("enc"), lax.axis_size("dec")
    me = lax.axis_index("enc") * dec + lax.axis_index("dec")

    def greet(d, _):
        other = lax.rem(me + d, enc * dec)
        pl.semaphore_signal(
            barrier, inc=1, device_id=(other // dec, lax.rem(other, dec)),
            device_id_type=pl.DeviceIdType.MESH,
        )
        return 0

    lax.fori_loop(1, enc * dec, greet, 0)
    pl.semaphore_wait(barrier, enc * dec - 1)


def remote(src, dst, send, recv, target):
    return pltpu.make_async_remote_copy(
        src_ref=src, dst_ref=dst, send_sem=send, recv_sem=recv,
        device_id=target, device_id_type=pl.DeviceIdType.MESH,
    )


def rows_of(ref, index, count):
    return ref.at[pl.ds(index * count, count), :]


def lanes(ref, index, width):
    return ref.at[:, pl.ds(pl.multiple_of(index * width, width), width)]


ORDER = (0, 1, 2, 4, 5, 6, 3, 7)


def partner(x, p):
    if isinstance(p, int):
        return flip(x, ORDER[p])
    d = jnp.int32(ORDER[0])
    for i, other in enumerate(ORDER):
        d = jnp.where(p == i, other, d)
    return flip(x, d)


def flip(x, d):
    parts = [lax.rem(lax.div(x, b) + lax.div(jnp.int32(d), b), 2) * b for b in (1, 2, 4)]
    return parts[0] + parts[1] + parts[2]


def fused_kernel(
    q, g, k, v, bias, ctx_o, dq_o, dk_o, dv_o,
    q_mid, g_mid, q_in, g_in, k_in, v_in, bias_in, kl, vl, kt, vt, qt, gt,
    s_buf, top_buf, e_buf, m_buf, m_run, o_acc, inv_buf, term_buf, dq_acc, dk_acc, dv_acc,
    cell_out, ctx_out, dq_out,
    mid_send, mid_recv, tok_send, tok_recv, bias_send, bias_recv, cell_send, cell_recv,
    grad_send, grad_recv, back_send, back_recv, local,
):
    enc, dec = lax.axis_size("enc"), lax.axis_size("dec")
    per = enc // dec
    e, z = lax.axis_index("enc"), lax.axis_index("dec")
    home, core = lax.div(e, per), lax.rem(e, per)
    cells, width = k_in.shape[1], k_in.shape[2]
    tok = q_in.shape[1]
    heads = width // DH
    piece = cells // 2
    parts = [slice(i * piece, (i + 1) * piece) for i in range(2 * cells // piece)]
    bf, f32 = jnp.bfloat16, jnp.float32
    near = lambda x: lax.rem(x, per) * dec + lax.div(x, per)
    slot = lambda x: z * enc + near(x)
    mine = home == z
    tokens = ((q, q_mid, q_in), (g, g_mid, g_in))
    greet_all()

    def plane_copy(n, d):
        src, mid, dst = tokens[n]
        i = lax.rem(home + d, dec)
        return remote(
            lanes(src, i, width), mid.at[home], mid_send.at[n, d], mid_recv.at[n, d],
            (per * i + core, z),
        )

    def pass_on(n, d, act):
        src, mid, dst = tokens[n]
        j = lax.rem(home - d + dec, dec)
        piece = lanes(src, home, width) if d == 0 else mid.at[j]
        here = dst.at[z]

        @pl.when(j == z)
        def _():
            act(pltpu.make_async_copy(piece, here, local.at[n]), True)

        @pl.when(j != z)
        def _():
            act(remote(piece, here, tok_send.at[n, d], tok_recv.at[n, z], (e, j)), False)

    def begin(copy, stays):
        copy.start()

    def finish(copy, stays):
        if not stays:
            copy.wait_send()

    def token_start(n):
        for d in range(1, dec):
            plane_copy(n, d).start()
        pass_on(n, 0, begin)

    def token_turn(n):
        src, mid, dst = tokens[n]
        for d in range(1, dec):
            j = lax.rem(home - d + dec, dec)
            remote(
                lanes(src, 0, width), mid.at[j], mid_send.at[n, d], mid_recv.at[n, d],
                (per * j + core, z),
            ).wait_recv()
            pass_on(n, d, begin)

    def token_ready(n, t):
        src, mid, dst = tokens[n]

        @pl.when(t == z)
        def _():
            pltpu.make_async_copy(lanes(src, home, width), dst.at[z], local.at[n]).wait()

        @pl.when(t != z)
        def _():
            remote(
                lanes(src, 0, width), dst.at[t], tok_send.at[n, 0], tok_recv.at[n, t], (e, t)
            ).wait_recv()

    def token_sent(n):
        for d in range(1, dec):
            plane_copy(n, d).wait_send()
        for d in range(dec):
            pass_on(n, d, finish)

    def bias_copy(i):
        return remote(
            bias, bias_in.at[z], bias_send.at[i], bias_recv.at[z], (e, lax.rem(z + i, dec))
        )

    bias_local = pltpu.make_async_copy(bias, bias_in.at[z], local.at[2])

    def bias_ready(t):
        pl.when(t == z)(lambda: bias_local.wait())

        @pl.when(t != z)
        def _():
            remote(bias, bias_in.at[t], bias_send.at[0], bias_recv.at[t], (e, z)).wait_recv()

    def cell_copy(n, src, dst, d):
        other = partner(e, d)
        return remote(
            lanes(src, slot(other), width), dst.at[d], cell_send.at[n, d], cell_recv.at[n, d],
            (other, z),
        )

    def cell_local(n, src, dst):
        return pltpu.make_async_copy(lanes(src, slot(e), width), dst.at[0], local.at[3 + n])

    def grad_copy(n, dst, d):
        other = partner(e, d)
        return remote(
            cell_out.at[n, d], lanes(dst, near(e), width), grad_send.at[n, d],
            grad_recv.at[n, d], (other, z),
        )

    def grad_wait(n, dst, d):
        other = partner(e, d)
        return remote(
            cell_out.at[n, d], lanes(dst, near(other), width), grad_send.at[n, d],
            grad_recv.at[n, d], (other, z),
        )

    def grad_local(n, dst):
        return pltpu.make_async_copy(
            cell_out.at[n, 0], lanes(dst, near(e), width), local.at[5 + n]
        )

    def back_copy(n, src, dst, t):
        return remote(
            src.at[t], lanes(dst, home, width), back_send.at[n, t], back_recv.at[n, home],
            (per * z + core, t),
        )

    def back_local(n, src, dst):
        return pltpu.make_async_copy(src.at[z], lanes(dst, home, width), local.at[7 + n])

    def back_start(n, src, dst, t):
        here = mine & (t == z)
        pl.when(here)(lambda: back_local(n, src, dst).start())
        pl.when(jnp.logical_not(here))(lambda: back_copy(n, src, dst, t).start())

    def back_finish(n, src, dst):
        for t in range(dec):
            here = mine & (t == z)
            pl.when(here)(lambda: back_local(n, src, dst).wait())
            pl.when(jnp.logical_not(here))(lambda: back_copy(n, src, dst, t).wait_send())
        for i in range(dec):

            @pl.when(jnp.logical_not(mine & (home == i)))
            def _():
                remote(
                    src.at[0], lanes(dst, i, width), back_send.at[n, 0], back_recv.at[n, i],
                    (e, z),
                ).wait_recv()

    token_start(0)
    for i in range(1, dec):
        bias_copy(i).start()
    bias_local.start()
    for n, src, dst in ((0, k, k_in), (1, v, v_in)):
        cell_local(n, src, dst).start()
        cell_copy(n, src, dst, 1).start()
    for d in range(2, enc):
        cell_copy(0, k, k_in, d).start()
        cell_copy(1, v, v_in, d).start()
        if d == 3:
            token_start(1)

    m_run[...] = jnp.full(m_run.shape, -3e38, f32)
    o_acc[...] = jnp.zeros(o_acc.shape, f32)
    dq_acc[...] = jnp.zeros(dq_acc.shape, f32)

    def prepare_tokens(t):
        token_ready(0, t)
        bias_ready(t)
        turned = q_in[t].T
        hidden = bias_in[t]
        blank = jnp.zeros((DH - hidden.shape[0], tok), bf)
        qt[t, 0] = jnp.concatenate([turned[:DH], hidden, blank], axis=0)
        qt[t, 1] = jnp.concatenate([hidden, blank, turned[DH:]], axis=0)

    def prepare_chunk(c):
        for i in range(2):
            d = 2 * c + i
            at = slice(i * cells, (i + 1) * cells)
            kc, vc = k_in[d], v_in[d]
            lane = lax.broadcasted_iota(jnp.int32, (cells, width), 1)
            block = partner(e, d) * (cells // BLOCK) + lax.broadcasted_iota(
                jnp.int32, (cells, width), 0
            ) // BLOCK
            ones = jnp.where(
                lax.broadcasted_iota(jnp.int32, (16, cells), 0) == 0, 1.0, 0.0
            ).astype(bf)
            turned = vc.T
            for h in range(heads):
                own = (lane >= h * DH) & (lane < (h + 1) * DH)
                spare = lane - (heads - 1 - h) * DH
                kl[c, h, at, :] = jnp.where(own, kc, jnp.where(spare == block, 1.0, 0.0).astype(bf))
                pair = (spare == 0) | (spare == 1)
                vl[c, h, at, :] = jnp.where(own, vc, jnp.where(pair, 1.0, 0.0).astype(bf))
                vt[c, h, :, at] = jnp.concatenate([turned[h * DH : (h + 1) * DH], ones], axis=0)
            kt[c, :, at] = kc.T

    def score(c, t, h, part, top8):
        s = nn(kl[c, h, part, :], qt[t, h])
        s_buf[h, part, :] = s
        return jnp.maximum(top8, jnp.max(s.reshape(piece // 8, 8, tok), axis=0))

    def score_first(c, t, h):
        top8 = jnp.full((8, tok), -3e38, f32)
        for part in parts:
            top8 = score(c, t, h, part, top8)
        top_buf[h] = top8

    def weigh(c, t, h, c_next, t_next, h_next):
        top = jnp.max(top_buf[h], axis=0, keepdims=True)
        top8 = jnp.full((8, tok), -3e38, f32)
        out = None
        for part in parts:
            w = jnp.exp(s_buf[h, part, :] - top).astype(bf)
            e_buf[c, t, h, part, :] = w
            top8 = score(c_next, t_next, h_next, part, top8)
            o = nn(vt[c, h, :, part], w)
            out = o if out is None else out + o
        top_buf[h_next] = top8
        before = m_run[t, h, 0:1, :]
        now = jnp.maximum(before, top)
        o_acc[t, h] = o_acc[t, h] * jnp.exp(before - now) + out * jnp.exp(top - now)
        m_run[t, h] = jnp.broadcast_to(now, (8, tok))
        m_buf[c, t, h] = jnp.broadcast_to(top, (8, tok))

    def finish_tokens(t):
        token_ready(1, t)
        turned = g_in[t].T
        gt[t] = turned
        found = []
        for h in range(heads):
            inv = 1.0 / o_acc[t, h, DH : DH + 1, :]
            part = o_acc[t, h, :DH, :] * inv
            found.append(part)
            term = jnp.sum(turned[h * DH : (h + 1) * DH].astype(f32) * part, axis=0, keepdims=True)
            inv_buf[t, h] = jnp.broadcast_to(inv, (8, tok))
            term_buf[t, h] = jnp.broadcast_to(-term, (8, tok))
        ctx_out[t] = jnp.concatenate(found, axis=0).T.astype(bf)
        back_start(0, ctx_out, ctx_o, t)

    def backward(c, t):
        lane = lax.broadcasted_iota(jnp.int32, (tok, width), 1)
        own = [(lane >= h * DH) & (lane < (h + 1) * DH) for h in range(heads)]
        row = lax.broadcasted_iota(jnp.int32, (DH, tok), 0)
        scaled, right = [], []
        for h in range(heads):
            factor = jnp.exp(m_buf[c, t, h, 0:1, :] - m_run[t, h, 0:1, :]) * inv_buf[t, h, 0:1, :]
            gs = (gt[t, h * DH : (h + 1) * DH, :].astype(f32) * factor).astype(bf)
            term = term_buf[t, h, 0:1, :] * factor
            high = term.astype(bf).astype(f32)
            extra = jnp.where(row == 0, high, jnp.where(row == 1, term - high, 0.0)).astype(bf)
            scaled.append(gs)
            right.append(jnp.concatenate([gs, extra] if h == 0 else [extra, gs], axis=0))
        g_rows = jnp.concatenate(scaled, axis=0).T
        q_rows = q_in[t]
        g_all = jnp.concatenate([jnp.where(o, g_rows, jnp.zeros_like(g_rows)) for o in own], axis=0)
        q_all = jnp.concatenate([jnp.where(o, q_rows, jnp.zeros_like(q_rows)) for o in own], axis=0)
        dq = [None] * heads

        def front(part):
            ds_all, e_all = [], []
            for h in range(heads):
                w = e_buf[c, t, h, part, :]
                ds_all.append((w.astype(f32) * nn(vl[c, h, part, :], right[h])).astype(bf))
                e_all.append(w)
            return part, ds_all, e_all

        def back(part, ds_all, e_all):
            dv_acc[part, :] += nn(jnp.concatenate(e_all, axis=1), g_all)
            for h in range(heads):
                term = nn(kt[c, h * DH : (h + 1) * DH, part], ds_all[h])
                dq[h] = term if dq[h] is None else dq[h] + term
            dk_acc[part, :] += nn(jnp.concatenate(ds_all, axis=1), q_all)

        held = front(parts[0])
        for part in parts[1:]:
            ahead = front(part)
            back(*held)
            held = ahead
        back(*held)
        dq_acc[t] += jnp.concatenate(dq, axis=0)

    def each(count, step):
        lax.fori_loop(0, count, lambda i, _: (step(i), 0)[1], 0)

    def arrive(c):
        for d in (2 * c, 2 * c + 1):
            cell_copy(0, k, k_in, d).wait_recv()
            cell_copy(1, v, v_in, d).wait_recv()

    cell_local(0, k, k_in).wait()
    cell_local(1, v, v_in).wait()
    cell_copy(0, k, k_in, 1).wait_recv()
    cell_copy(1, v, v_in, 1).wait_recv()
    prepare_chunk(0)
    token_turn(0)
    prepare_tokens(z)
    score_first(0, z, 0)
    chunks = enc // 2
    last = chunks * dec - 1

    def ahead(n):
        c, i = lax.div(n, dec), lax.rem(n, dec)
        t = flip(z, i)
        m = jnp.minimum(n + 1, last)
        c_next, t_next = lax.div(m, dec), flip(z, lax.rem(m, dec))
        weigh(c, t, 0, c, t, 1)
        pl.when(n == 1)(lambda: token_turn(1))
        pl.when(n < dec - 1)(lambda: prepare_tokens(t_next))

        @pl.when((i == dec - 1) & (n < last))
        def _():
            arrive(c_next)
            prepare_chunk(c_next)

        weigh(c, t, 1, c_next, t_next, 0)
        pl.when(c == chunks - 1)(lambda: finish_tokens(t))

    each(last + 1, ahead)

    def clear():
        dk_acc[...] = jnp.zeros(dk_acc.shape, f32)
        dv_acc[...] = jnp.zeros(dv_acc.shape, f32)

    def keep(c):
        for i in range(2):
            at = slice(i * cells, (i + 1) * cells)
            cell_out[0, 2 * c + i] = dk_acc[at, :].astype(bf)
            cell_out[1, 2 * c + i] = dv_acc[at, :].astype(bf)

    def far_chunk(n):
        c = chunks - 1 - n
        clear()
        each(dec, lambda t: backward(c, t))
        keep(c)
        for i in range(2):
            grad_copy(0, dk_o, 2 * c + i).start()
            grad_copy(1, dv_o, 2 * c + i).start()

    each(chunks - 1, far_chunk)
    clear()

    def last_tokens(i):
        t = flip(z, dec - 1 - i)
        backward(0, t)
        dq_out[t] = dq_acc[t].T.astype(bf)
        back_start(1, dq_out, dq_o, t)

    each(dec, last_tokens)
    keep(0)
    for n, dst in ((0, dk_o), (1, dv_o)):
        grad_copy(n, dst, 1).start()
        grad_local(n, dst).start()

    token_sent(0)
    token_sent(1)
    for i in range(1, dec):
        bias_copy(i).wait_send()
    for d in range(1, enc):
        cell_copy(0, k, k_in, d).wait_send()
        cell_copy(1, v, v_in, d).wait_send()
    for n, dst in ((0, dk_o), (1, dv_o)):
        for d in range(1, enc):
            grad_copy(n, dst, d).wait_send()
            grad_wait(n, dst, d).wait_recv()
        grad_local(n, dst).wait()
    back_finish(0, ctx_out, ctx_o)
    back_finish(1, dq_out, dq_o)


def settle_kernel(*refs):
    src, dst, mid, sems = refs[:4], refs[4:8], refs[8:12], refs[12]
    steps = []
    for n, (a, m, b) in enumerate(zip(src, mid, dst)):
        for i in range(4):
            count = a.shape[0] // 4
            steps.append((
                pltpu.make_async_copy(rows_of(a, i, count), rows_of(m, i, count), sems.at[0, n, i]),
                pltpu.make_async_copy(rows_of(m, i, count), rows_of(b, i, count), sems.at[1, n, i]),
            ))
    for load, store in steps:
        load.start()
    for load, store in steps:
        load.wait()
        store.start()
    for load, store in steps:
        store.wait()


def settle(outs):
    return pl.pallas_call(
        settle_kernel,
        out_shape=[jax.ShapeDtypeStruct(x.shape, x.dtype) for x in outs],
        in_specs=[pl.BlockSpec(memory_space=pl.ANY)] * 4,
        out_specs=[pl.BlockSpec(memory_space=pl.ANY)] * 4,
        scratch_shapes=[pltpu.VMEM(x.shape, x.dtype) for x in outs]
        + [pltpu.SemaphoreType.DMA((2, 4, 4))],
        name="settle",
    )(*outs)


def fused(q, g, k, v, bias):
    enc, dec = lax.axis_size("enc"), lax.axis_size("dec")
    width = k.shape[1] // (enc * dec)
    heads = width // DH
    tok, chunk = q.shape[0], k.shape[0]
    bf, f32 = jnp.bfloat16, jnp.float32
    dma = pltpu.SemaphoreType.DMA
    vmem = pltpu.VMEM
    token_out = jax.ShapeDtypeStruct((tok, dec * width), bf)
    cell_out = jax.ShapeDtypeStruct((chunk, enc * width), bf)
    return pl.pallas_call(
        fused_kernel,
        out_shape=(token_out, token_out, cell_out, cell_out),
        in_specs=[pl.BlockSpec(memory_space=pl.ANY)] * 5,
        out_specs=[pl.BlockSpec(memory_space=pl.ANY)] * 4,
        scratch_shapes=[
            vmem((dec, tok, width), bf), vmem((dec, tok, width), bf),
            vmem((dec, tok, width), bf), vmem((dec, tok, width), bf),
            vmem((enc, chunk, width), bf), vmem((enc, chunk, width), bf),
            vmem((dec, bias.shape[0], tok), bf),
            vmem((enc // 2, heads, 2 * chunk, width), bf),
            vmem((enc // 2, heads, 2 * chunk, width), bf),
            vmem((enc // 2, width, 2 * chunk), bf),
            vmem((enc // 2, heads, DH + 16, 2 * chunk), bf),
            vmem((dec, heads, width, tok), bf), vmem((dec, width, tok), bf),
            vmem((heads, 2 * chunk, tok), f32), vmem((heads, 8, tok), f32),
            vmem((enc // 2, dec, heads, 2 * chunk, tok), bf),
            vmem((enc // 2, dec, heads, 8, tok), f32), vmem((dec, heads, 8, tok), f32),
            vmem((dec, heads, DH + 16, tok), f32),
            vmem((dec, heads, 8, tok), f32), vmem((dec, heads, 8, tok), f32),
            vmem((dec, width, tok), f32),
            vmem((2 * chunk, width), f32), vmem((2 * chunk, width), f32),
            vmem((2, enc, chunk, width), bf), vmem((dec, tok, width), bf),
            vmem((dec, tok, width), bf),
            dma((2, dec)), dma((2, dec)), dma((2, dec)), dma((2, dec)), dma((dec,)), dma((dec,)),
            dma((2, enc)), dma((2, enc)), dma((2, enc)), dma((2, enc)),
            dma((2, dec)), dma((2, dec)), dma((9,)),
        ],
        compiler_params=pltpu.CompilerParams(
            collective_id=0, has_side_effects=True, vmem_limit_bytes=60 * 1024 * 1024
        ),
        name="fused",
    )(q, g, k, v, bias)


def shared_head(q, g, k, v, bias, per, dec):
    share = DH // q.shape[1]
    mates = [
        [per * (j + i) + c for i in range(share)] for c in range(per) for j in range(0, dec, share)
    ]
    place = lax.rem(lax.axis_index("enc") // per, share)
    rows = q.shape[0] // share

    def to_head(x):
        return lax.all_to_all(x, "enc", 0, 1, axis_index_groups=mates, tiled=True)

    def from_head(x):
        return lax.all_to_all(x, "enc", 1, 0, axis_index_groups=mates, tiled=True)

    def widen(x):
        return lax.all_gather(x, "enc", axis=1, axis_index_groups=mates, tiled=True)

    def add_up(x):
        total = lax.psum_scatter(
            x, "enc", scatter_dimension=1, axis_index_groups=mates, tiled=True
        )
        return total.astype(jnp.bfloat16)

    bias = lax.dynamic_slice_in_dim(bias, place * rows, rows, 1)
    ctx, dq, dk, dv = attention(to_head(q), to_head(g), widen(k), widen(v), bias, jnp.float32)
    return from_head(ctx), from_head(dq), add_up(dk), add_up(dv)


def body(queries, out_grad, memory_keys, memory_values, ref_blocks, ref_counts):
    enc, dec = lax.axis_size("enc"), lax.axis_size("dec")
    per = enc // dec
    tok, tok_width = queries.shape
    own_cells, full = memory_keys.shape
    width = full // (enc * dec)
    groups = [[per * k + c for k in range(dec)] for c in range(per)]

    def token_in(x):
        x = x.reshape(tok, dec, width).transpose(1, 0, 2)
        x = lax.all_to_all(x, "enc", 0, 0, axis_index_groups=groups)
        return lax.all_to_all(x, "dec", 0, 0).reshape(dec * tok, width)

    def token_out(x):
        x = lax.all_to_all(x.reshape(dec, tok, width), "dec", 0, 0)
        x = lax.all_to_all(x, "enc", 0, 0, axis_index_groups=groups)
        return x.transpose(1, 0, 2).reshape(tok, tok_width)

    def cell_in(x):
        x = lax.dynamic_slice_in_dim(x, lax.axis_index("dec") * (full // dec), full // dec, 1)
        x = x.reshape(own_cells, per, dec, width).transpose(2, 1, 0, 3)
        x = lax.all_to_all(x.reshape(enc, own_cells, width), "enc", 0, 0)
        return x.reshape(enc * own_cells, width)

    def cell_out(x):
        x = lax.all_to_all(x.reshape(enc, own_cells, width), "enc", 0, 0)
        x = x.reshape(dec, per, own_cells, width).transpose(2, 1, 0, 3)
        return x.reshape(own_cells, full // dec)

    bias = hidden_blocks(ref_blocks, ref_counts, enc * own_cells // BLOCK)
    small = enc * own_cells // BLOCK <= DH
    if width == LANES and enc == 8 and dec == 4 and small:
        return tuple(settle(fused(queries, out_grad, memory_keys, memory_values, bias)))
    bias = lax.all_gather(bias, "dec", axis=1, tiled=True)
    q, g, k, v = token_in(queries), token_in(out_grad), cell_in(memory_keys), cell_in(memory_values)
    if width >= DH:
        ctx, dq, dk, dv = attention(q, g, k, v, bias)
    else:
        ctx, dq, dk, dv = shared_head(q, g, k, v, bias, per, dec)
    return token_out(ctx), token_out(dq), cell_out(dk), cell_out(dv)


def solution(mesh):
    in_specs = (
        P("dec", "enc"),
        P("dec", "enc"),
        P("enc", None),
        P("enc", None),
        P("dec", None),
        P("dec"),
    )
    out_specs = (P("dec", "enc"), P("dec", "enc"), P("enc", "dec"), P("enc", "dec"))
    return jax.shard_map(body, mesh=mesh, in_specs=in_specs, out_specs=out_specs, check_vma=False)
```

```python
import functools

import jax
import jax.numpy as jnp
import numpy as np
from jax import lax
from jax.experimental import pallas as pl
from jax.experimental.pallas import tpu as pltpu
from jax.sharding import PartitionSpec as P

DH = 64
BLOCK = 128
HIDDEN = -1e30
LANES = 128


def nt(a, b):
    return lax.dot_general(a, b, (((1,), (1,)), ((), ())), preferred_element_type=jnp.float32)


def nn(a, b):
    return lax.dot_general(a, b, (((1,), (0,)), ((), ())), preferred_element_type=jnp.float32)


def attention_kernel(
    heads, chunk, k_ref, v_ref, e_ref, q_ref, g_ref, bias_ref,
    ctx_ref, dq_ref, dk_ref, dv_ref,
    kt, vt, s_buf, e_buf, dk_acc, dv_acc,
):
    step = pl.program_id(0)
    cells, width = k_ref.shape
    rows = q_ref.shape[0]
    chunks = cells // chunk

    @pl.when(step == 0)
    def _():
        def prepare(i, _):
            at = pl.ds(pl.multiple_of(i * chunk, chunk), chunk)
            kt[:, at] = k_ref[at, :].T
            vt[:, at] = v_ref[at, :].T
            dk_acc[at, :] = jnp.zeros((chunk, width), jnp.float32)
            dv_acc[at, :] = jnp.zeros((chunk, width), jnp.float32)
            return 0

        lax.fori_loop(0, chunks, prepare, 0)

    lane = lax.broadcasted_iota(jnp.int32, (rows, width), 1)
    own = [(lane >= h * DH) & (lane < (h + 1) * DH) for h in range(heads)]
    q = q_ref[...]
    q_own = [jnp.where(own[h], q, jnp.zeros_like(q)) for h in range(heads)]
    bias = bias_ref[...].astype(jnp.float32)
    blank = jnp.zeros((LANES - bias.shape[0], rows), jnp.float32)
    bias = jnp.concatenate([bias, blank], axis=0).T.astype(jnp.bfloat16)
    q_aug = [jnp.concatenate([q_own[h], bias], axis=1) for h in range(heads)]

    def score_chunk(i, tops):
        at = pl.ds(pl.multiple_of(i * chunk, chunk), chunk)
        left = jnp.concatenate([k_ref[at, :], e_ref[at, :]], axis=1)
        out = []
        for h in range(heads):
            s = nt(left, q_aug[h])
            s_buf[h, at, :] = s
            out.append(jnp.maximum(tops[h], jnp.max(s.reshape(chunk // 8, 8, rows), axis=0)))
        return tuple(out)

    tops = lax.fori_loop(
        0, chunks, score_chunk, tuple(jnp.full((8, rows), -3e38, jnp.float32) for _ in range(heads))
    )
    top = [jnp.max(t, axis=0, keepdims=True) for t in tops]

    def weight_chunk(i, carry):
        at = pl.ds(pl.multiple_of(i * chunk, chunk), chunk)
        totals, outs = carry
        new_totals, new_outs = [], []
        for h in range(heads):
            e = jnp.exp(s_buf[h, at, :] - top[h])
            new_totals.append(totals[h] + jnp.sum(e.reshape(chunk // 8, 8, rows), axis=0))
            e = e.astype(jnp.bfloat16)
            e_buf[h, at, :] = e
            new_outs.append(outs[h] + nn(vt[h * DH : (h + 1) * DH, at], e))
        return tuple(new_totals), tuple(new_outs)

    totals, outs = lax.fori_loop(
        0,
        chunks,
        weight_chunk,
        (
            tuple(jnp.zeros((8, rows), jnp.float32) for _ in range(heads)),
            tuple(jnp.zeros((DH, rows), jnp.float32) for _ in range(heads)),
        ),
    )
    inv = [1.0 / jnp.sum(t, axis=0, keepdims=True) for t in totals]
    stack = jnp.concatenate(
        [outs[h] * inv[h] for h in range(heads)]
        + [jnp.broadcast_to(inv[h], (DH, rows)) for h in range(heads)],
        axis=0,
    ).T
    attended = stack[:, :width]
    ctx_ref[...] = attended.astype(ctx_ref.dtype)
    g_scaled = (g_ref[...].astype(jnp.float32) * stack[:, width:]).astype(jnp.bfloat16)
    product = g_scaled.astype(jnp.float32) * attended
    lane_aug = lax.broadcasted_iota(jnp.int32, (rows, LANES), 1)
    g_own, g_aug = [], []
    for h in range(heads):
        term = -jnp.sum(jnp.where(own[h], product, 0.0), axis=1, keepdims=True)
        high = term.astype(jnp.bfloat16).astype(jnp.float32)
        low = term - high
        extra = jnp.where(
            lane_aug == LANES - 1, high, jnp.where(lane_aug == LANES - 2, low, 0.0)
        ).astype(jnp.bfloat16)
        g_own.append(jnp.where(own[h], g_scaled, jnp.zeros_like(g_scaled)))
        g_aug.append(jnp.concatenate([g_own[h], extra], axis=1))
    q_all = jnp.concatenate(q_own, axis=0)
    g_all = jnp.concatenate(g_own, axis=0)

    def grad_chunk(i, dqs):
        at = pl.ds(pl.multiple_of(i * chunk, chunk), chunk)
        left = jnp.concatenate([v_ref[at, :], e_ref[at, :]], axis=1)
        new_dqs, ds_all, e_all = [], [], []
        for h in range(heads):
            e = e_buf[h, at, :]
            ds = (e.astype(jnp.float32) * nt(left, g_aug[h])).astype(jnp.bfloat16)
            new_dqs.append(dqs[h] + nn(kt[h * DH : (h + 1) * DH, at], ds))
            ds_all.append(ds)
            e_all.append(e)
        dk_acc[at, :] += nn(jnp.concatenate(ds_all, axis=1), q_all)
        dv_acc[at, :] += nn(jnp.concatenate(e_all, axis=1), g_all)
        return tuple(new_dqs)

    dqs = lax.fori_loop(
        0, chunks, grad_chunk, tuple(jnp.zeros((DH, rows), jnp.float32) for _ in range(heads))
    )
    dq_ref[...] = jnp.concatenate(dqs, axis=0).T.astype(dq_ref.dtype)

    @pl.when(step == pl.num_programs(0) - 1)
    def _():
        dk_ref[...] = dk_acc[...].astype(dk_ref.dtype)
        dv_ref[...] = dv_acc[...].astype(dv_ref.dtype)


def cell_marks(cells):
    block_ids = lax.broadcasted_iota(jnp.int32, (cells, LANES), 0) // BLOCK
    lane = lax.broadcasted_iota(jnp.int32, (cells, LANES), 1)
    return ((block_ids == lane) | (lane >= LANES - 2)).astype(jnp.bfloat16)


def attention(q, g, k, v, bias, grad_type=jnp.bfloat16, rows=512, chunk=2048):
    tokens, width = q.shape
    cells = k.shape[0]
    heads = width // DH
    chunk = min(chunk, cells)
    whole = lambda i: (0, 0)
    part = lambda i: (i, 0)
    cell_spec = pl.BlockSpec((cells, width), whole)
    token_spec = pl.BlockSpec((rows, width), part)
    bf = jnp.bfloat16
    return pl.pallas_call(
        functools.partial(attention_kernel, heads, chunk),
        grid=(tokens // rows,),
        out_shape=(
            jax.ShapeDtypeStruct((tokens, width), bf),
            jax.ShapeDtypeStruct((tokens, width), bf),
            jax.ShapeDtypeStruct((cells, width), grad_type),
            jax.ShapeDtypeStruct((cells, width), grad_type),
        ),
        in_specs=[
            cell_spec,
            cell_spec,
            pl.BlockSpec((cells, LANES), whole),
            token_spec,
            token_spec,
            pl.BlockSpec((bias.shape[0], rows), lambda i: (0, i)),
        ],
        out_specs=(token_spec, token_spec, cell_spec, cell_spec),
        scratch_shapes=[
            pltpu.VMEM((width, cells), bf),
            pltpu.VMEM((width, cells), bf),
            pltpu.VMEM((heads, cells, rows), jnp.float32),
            pltpu.VMEM((heads, cells, rows), bf),
            pltpu.VMEM((cells, width), jnp.float32),
            pltpu.VMEM((cells, width), jnp.float32),
        ],
        compiler_params=pltpu.CompilerParams(vmem_limit_bytes=60 * 1024 * 1024),
        name="attention",
    )(k, v, cell_marks(cells), q, g, bias)


def hidden_blocks(ref_blocks, ref_counts, blocks):
    slot_ids = jnp.arange(ref_blocks.shape[1], dtype=jnp.int32)
    live = slot_ids[None, :] < ref_counts[:, None]
    wanted = jnp.where(live, ref_blocks, -1).T
    seen = jnp.any(wanted[:, None, :] == jnp.arange(blocks, dtype=jnp.int32)[:, None], axis=0)
    return jnp.where(seen, 0.0, HIDDEN).astype(jnp.bfloat16)


def greet():
    barrier = pltpu.get_barrier_semaphore()
    enc, dec = lax.axis_size("enc"), lax.axis_size("dec")
    per = enc // dec
    e, z = lax.axis_index("enc"), lax.axis_index("dec")
    home, core = lax.div(e, per), lax.rem(e, per)

    def signal(target):
        pl.semaphore_signal(
            barrier, inc=1, device_id=target, device_id_type=pl.DeviceIdType.MESH
        )

    for d in range(1, dec):
        signal((e, lax.rem(z + d, dec)))
    for i in range(dec):
        pl.when((home != z) & (home != i))(lambda: signal((per * i + core, home)))
    for d in range(1, enc):
        signal((flip(e, d), z))
    away = jnp.where(home == z, 0, dec - 1)
    pl.semaphore_wait(barrier, enc + dec - 2 + away)


def remote(src, dst, send, recv, target):
    return pltpu.make_async_remote_copy(
        src_ref=src, dst_ref=dst, send_sem=send, recv_sem=recv,
        device_id=target, device_id_type=pl.DeviceIdType.MESH,
    )


def rows_of(ref, index, count):
    return ref.at[pl.ds(index * count, count), :]


def lanes(ref, index, width):
    return ref.at[:, pl.ds(pl.multiple_of(index * width, width), width)]


ORDER = (0, 1, 2, 4, 5, 6, 3, 7)


def partner(x, p):
    if isinstance(p, int):
        return flip(x, ORDER[p])
    d = jnp.int32(ORDER[0])
    for i, other in enumerate(ORDER):
        d = jnp.where(p == i, other, d)
    return flip(x, d)


def flip(x, d):
    parts = [lax.rem(lax.div(x, b) + lax.div(jnp.int32(d), b), 2) * b for b in (1, 2, 4)]
    return parts[0] + parts[1] + parts[2]


def fused_kernel(
    q, g, k, v, bias, ctx_o, dq_o, dk_o, dv_o,
    q_mid, g_mid, q_in, g_in, k_in, v_in, bias_in, kl, vl, kt, vt, qt, gt,
    s_buf, top_buf, e_buf, m_buf, m_run, o_acc, inv_buf, term_buf, dq_acc, dk_acc, dv_acc,
    cell_out, ctx_out, dq_out,
    mid_send, mid_recv, tok_send, tok_recv, bias_send, bias_recv, cell_send, cell_recv,
    grad_send, grad_recv, back_send, back_recv, local,
):
    enc, dec = lax.axis_size("enc"), lax.axis_size("dec")
    per = enc // dec
    e, z = lax.axis_index("enc"), lax.axis_index("dec")
    home, core = lax.div(e, per), lax.rem(e, per)
    cells, width = k_in.shape[1], k_in.shape[2]
    tok = q_in.shape[1]
    heads = width // DH
    piece = cells // 2
    parts = [slice(i * piece, (i + 1) * piece) for i in range(2 * cells // piece)]
    bf, f32 = jnp.bfloat16, jnp.float32
    near = lambda x: lax.rem(x, per) * dec + lax.div(x, per)
    slot = lambda x: z * enc + near(x)
    mine = home == z
    tokens = ((q, q_mid, q_in), (g, g_mid, g_in))
    greet()

    def plane_copy(n, d):
        src, mid, dst = tokens[n]
        i = lax.rem(home + d, dec)
        return remote(
            lanes(src, i, width), mid.at[home], mid_send.at[n, d], mid_recv.at[n, d],
            (per * i + core, z),
        )

    def pass_on(n, d, act):
        src, mid, dst = tokens[n]
        j = lax.rem(home - d + dec, dec)
        piece = lanes(src, home, width) if d == 0 else mid.at[j]
        here = dst.at[z]

        @pl.when(j == z)
        def _():
            act(pltpu.make_async_copy(piece, here, local.at[n]), True)

        @pl.when(j != z)
        def _():
            act(remote(piece, here, tok_send.at[n, d], tok_recv.at[n, z], (e, j)), False)

    def begin(copy, stays):
        copy.start()

    def finish(copy, stays):
        if not stays:
            copy.wait_send()

    def token_start(n):
        for d in range(1, dec):
            plane_copy(n, d).start()
        pass_on(n, 0, begin)

    def token_turn(n):
        src, mid, dst = tokens[n]
        for d in range(1, dec):
            j = lax.rem(home - d + dec, dec)
            remote(
                lanes(src, 0, width), mid.at[j], mid_send.at[n, d], mid_recv.at[n, d],
                (per * j + core, z),
            ).wait_recv()
            pass_on(n, d, begin)

    def token_ready(n, t):
        src, mid, dst = tokens[n]

        @pl.when(t == z)
        def _():
            pltpu.make_async_copy(lanes(src, home, width), dst.at[z], local.at[n]).wait()

        @pl.when(t != z)
        def _():
            remote(
                lanes(src, 0, width), dst.at[t], tok_send.at[n, 0], tok_recv.at[n, t], (e, t)
            ).wait_recv()

    def token_sent(n):
        for d in range(1, dec):
            plane_copy(n, d).wait_send()
        for d in range(dec):
            pass_on(n, d, finish)

    def bias_copy(i):
        return remote(
            bias, bias_in.at[z], bias_send.at[i], bias_recv.at[z], (e, lax.rem(z + i, dec))
        )

    bias_local = pltpu.make_async_copy(bias, bias_in.at[z], local.at[2])

    def bias_ready(t):
        pl.when(t == z)(lambda: bias_local.wait())

        @pl.when(t != z)
        def _():
            remote(bias, bias_in.at[t], bias_send.at[0], bias_recv.at[t], (e, z)).wait_recv()

    def cell_copy(n, src, dst, d):
        other = partner(e, d)
        return remote(
            lanes(src, slot(other), width), dst.at[d], cell_send.at[n, d], cell_recv.at[n, d],
            (other, z),
        )

    def cell_local(n, src, dst):
        return pltpu.make_async_copy(lanes(src, slot(e), width), dst.at[0], local.at[3 + n])

    def grad_copy(n, dst, d):
        other = partner(e, d)
        return remote(
            cell_out.at[n, d], lanes(dst, near(e), width), grad_send.at[n, d],
            grad_recv.at[n, d], (other, z),
        )

    def grad_wait(n, dst, d):
        other = partner(e, d)
        return remote(
            cell_out.at[n, d], lanes(dst, near(other), width), grad_send.at[n, d],
            grad_recv.at[n, d], (other, z),
        )

    def grad_local(n, dst):
        return pltpu.make_async_copy(
            cell_out.at[n, 0], lanes(dst, near(e), width), local.at[5 + n]
        )

    def back_copy(n, src, dst, t):
        return remote(
            src.at[t], lanes(dst, home, width), back_send.at[n, t], back_recv.at[n, home],
            (per * z + core, t),
        )

    def back_local(n, src, dst):
        return pltpu.make_async_copy(src.at[z], lanes(dst, home, width), local.at[7 + n])

    def back_start(n, src, dst, t):
        here = mine & (t == z)
        pl.when(here)(lambda: back_local(n, src, dst).start())
        pl.when(jnp.logical_not(here))(lambda: back_copy(n, src, dst, t).start())

    def back_finish(n, src, dst):
        for t in range(dec):
            here = mine & (t == z)
            pl.when(here)(lambda: back_local(n, src, dst).wait())
            pl.when(jnp.logical_not(here))(lambda: back_copy(n, src, dst, t).wait_send())
        for i in range(dec):

            @pl.when(jnp.logical_not(mine & (home == i)))
            def _():
                remote(
                    src.at[0], lanes(dst, i, width), back_send.at[n, 0], back_recv.at[n, i],
                    (e, z),
                ).wait_recv()

    token_start(0)
    for i in range(1, dec):
        bias_copy(i).start()
    bias_local.start()
    for n, src, dst in ((0, k, k_in), (1, v, v_in)):
        cell_local(n, src, dst).start()
        cell_copy(n, src, dst, 1).start()
    for d in range(2, enc):
        cell_copy(0, k, k_in, d).start()
        cell_copy(1, v, v_in, d).start()
        if d == 3:
            token_start(1)

    m_run[...] = jnp.full(m_run.shape, -3e38, f32)
    o_acc[...] = jnp.zeros(o_acc.shape, f32)
    dq_acc[...] = jnp.zeros(dq_acc.shape, f32)

    def prepare_tokens(t):
        token_ready(0, t)
        bias_ready(t)
        turned = q_in[t].T
        hidden = bias_in[t]
        blank = jnp.zeros((DH - hidden.shape[0], tok), bf)
        qt[t, 0] = jnp.concatenate([turned[:DH], hidden, blank], axis=0)
        qt[t, 1] = jnp.concatenate([hidden, blank, turned[DH:]], axis=0)

    def prepare_cells(c, i):
        d = 2 * c + i
        at = slice(i * cells, (i + 1) * cells)
        kc, vc = k_in[d], v_in[d]
        lane = lax.broadcasted_iota(jnp.int32, (cells, width), 1)
        block = partner(e, d) * (cells // BLOCK) + lax.broadcasted_iota(
            jnp.int32, (cells, width), 0
        ) // BLOCK
        ones = jnp.where(
            lax.broadcasted_iota(jnp.int32, (16, cells), 0) == 0, 1.0, 0.0
        ).astype(bf)
        turned = vc.T
        for h in range(heads):
            own = (lane >= h * DH) & (lane < (h + 1) * DH)
            spare = lane - (heads - 1 - h) * DH
            kl[c, h, at, :] = jnp.where(own, kc, jnp.where(spare == block, 1.0, 0.0).astype(bf))
            pair = (spare == 0) | (spare == 1)
            vl[c, h, at, :] = jnp.where(own, vc, jnp.where(pair, 1.0, 0.0).astype(bf))
            vt[c, h, :, at] = jnp.concatenate([turned[h * DH : (h + 1) * DH], ones], axis=0)
        kt[c, :, at] = kc.T

    def score(c, t, h, part, top8):
        s = nn(kl[c, h, part, :], qt[t, h])
        s_buf[h, part, :] = s
        return jnp.maximum(top8, jnp.max(s.reshape(piece // 8, 8, tok), axis=0))

    def score_first(c, t, h):
        top8 = jnp.full((8, tok), -3e38, f32)
        for part in parts:
            top8 = score(c, t, h, part, top8)
        top_buf[h] = top8

    def weigh(c, t, h, c_next, t_next, h_next):
        top = jnp.max(top_buf[h], axis=0, keepdims=True)
        top8 = jnp.full((8, tok), -3e38, f32)
        out = None
        for part in parts:
            w = jnp.exp(s_buf[h, part, :] - top).astype(bf)
            e_buf[c, t, h, part, :] = w
            top8 = score(c_next, t_next, h_next, part, top8)
            o = nn(vt[c, h, :, part], w)
            out = o if out is None else out + o
        top_buf[h_next] = top8
        before = m_run[t, h, 0:1, :]
        now = jnp.maximum(before, top)
        o_acc[t, h] = o_acc[t, h] * jnp.exp(before - now) + out * jnp.exp(top - now)
        m_run[t, h] = jnp.broadcast_to(now, (8, tok))
        m_buf[c, t, h] = jnp.broadcast_to(top, (8, tok))

    def finish_tokens(t):
        token_ready(1, t)
        turned = g_in[t].T
        gt[t] = turned
        found = []
        for h in range(heads):
            inv = 1.0 / o_acc[t, h, DH : DH + 1, :]
            part = o_acc[t, h, :DH, :] * inv
            found.append(part)
            term = jnp.sum(turned[h * DH : (h + 1) * DH].astype(f32) * part, axis=0, keepdims=True)
            inv_buf[t, h] = jnp.broadcast_to(inv, (8, tok))
            term_buf[t, h] = jnp.broadcast_to(-term, (8, tok))
        ctx_out[t] = jnp.concatenate(found, axis=0).T.astype(bf)
        back_start(0, ctx_out, ctx_o, t)

    lane = lax.broadcasted_iota(jnp.int32, (tok, width), 1)
    own = [(lane >= h * DH) & (lane < (h + 1) * DH) for h in range(heads)]

    def apart(x):
        return jnp.concatenate([jnp.where(o, x, jnp.zeros_like(x)) for o in own], axis=0)

    def scale(c, t, h):
        factor = jnp.exp(m_buf[c, t, h, 0:1, :] - m_run[t, h, 0:1, :]) * inv_buf[t, h, 0:1, :]
        return factor, (gt[t, h * DH : (h + 1) * DH, :].astype(f32) * factor).astype(bf)

    def with_term(t, h, factor, gs):
        row = lax.broadcasted_iota(jnp.int32, (DH, tok), 0)
        term = term_buf[t, h, 0:1, :] * factor
        high = term.astype(bf).astype(f32)
        extra = jnp.where(row == 0, high, jnp.where(row == 1, term - high, 0.0)).astype(bf)
        return jnp.concatenate([gs, extra] if h == 0 else [extra, gs], axis=0)

    def score_grad(c, t, h, part, right):
        w = e_buf[c, t, h, part, :]
        return w, (w.astype(f32) * nn(vl[c, h, part, :], right)).astype(bf)

    def query_term(c, h, part, ds):
        return nn(kt[c, h * DH : (h + 1) * DH, part], ds)

    def backward(c, t, parts=parts):
        scaled = [scale(c, t, h) for h in range(heads)]
        right = [with_term(t, h, *scaled[h]) for h in range(heads)]
        g_all = apart(jnp.concatenate([gs for _, gs in scaled], axis=0).T)
        q_all = apart(q_in[t])
        dq = [None] * heads

        def front(part):
            return part, [score_grad(c, t, h, part, right[h]) for h in range(heads)]

        def back(part, pairs):
            dv_acc[part, :] += nn(jnp.concatenate([w for w, _ in pairs], axis=1), g_all)
            for h in range(heads):
                term = query_term(c, h, part, pairs[h][1])
                dq[h] = term if dq[h] is None else dq[h] + term
            dk_acc[part, :] += nn(jnp.concatenate([ds for _, ds in pairs], axis=1), q_all)

        held = front(parts[0])
        for part in parts[1:]:
            following = front(part)
            back(*held)
            held = following
        back(*held)
        dq_acc[t] += jnp.concatenate(dq, axis=0)

    def backward_queries(t, count):
        dq = [None] * heads
        rights = [[with_term(t, h, *scale(c, t, h)) for h in range(heads)] for c in range(count)]

        def back(c, part, grads):
            for h in range(heads):
                e_buf[c + 2, t, h, part, :] = grads[h]
                term = query_term(c, h, part, grads[h])
                dq[h] = term if dq[h] is None else dq[h] + term

        held = None
        for c in range(count):
            for part in parts:
                grads = [score_grad(c, t, h, part, rights[c][h])[1] for h in range(heads)]
                if held is not None:
                    back(*held)
                held = (c, part, grads)
        back(*held)
        dq_out[t] = (dq_acc[t] + jnp.concatenate(dq, axis=0)).T.astype(bf)

    def value_cells(c, t):
        g_all = apart(jnp.concatenate([scale(c, t, h)[1] for h in range(heads)], axis=0).T)
        for half in (slice(0, cells), slice(cells, 2 * cells)):
            dv_acc[half, :] += nn(
                jnp.concatenate([e_buf[c, t, h, half, :] for h in range(heads)], axis=1), g_all
            )

    def key_cells(c, t):
        q_all = apart(q_in[t])
        for half in (slice(0, cells), slice(cells, 2 * cells)):
            dk_acc[half, :] += nn(
                jnp.concatenate([e_buf[c + 2, t, h, half, :] for h in range(heads)], axis=1), q_all
            )

    def backward_cells(c, t):
        value_cells(c, t)
        key_cells(c, t)

    def each(count, step):
        lax.fori_loop(0, count, lambda i, _: (step(i), 0)[1], 0)

    def arrive(d):
        cell_copy(0, k, k_in, d).wait_recv()
        cell_copy(1, v, v_in, d).wait_recv()

    cell_local(0, k, k_in).wait()
    cell_local(1, v, v_in).wait()
    prepare_cells(0, 0)
    token_turn(0)
    arrive(1)
    prepare_cells(0, 1)
    prepare_tokens(z)
    score_first(0, z, 0)
    chunks = enc // 2
    last = chunks * dec - 1

    spread = flip(z, home)

    def turn(n):
        c, i = lax.div(n, dec), lax.rem(n, dec)
        return c, flip(jnp.where(c == 0, z, spread), i)

    def ahead(n):
        i = lax.rem(n, dec)
        c, t = turn(n)
        c_next, t_next = turn(jnp.minimum(n + 1, last))
        weigh(c, t, 0, c, t, 1)
        pl.when(n == 1)(lambda: token_turn(1))
        pl.when(n < dec - 1)(lambda: prepare_tokens(t_next))

        @pl.when((i == dec - 1) & (n < last))
        def _():
            for i in range(2):
                arrive(2 * c_next + i)
                prepare_cells(c_next, i)

        weigh(c, t, 1, c_next, t_next, 0)
        pl.when(c == chunks - 1)(lambda: finish_tokens(t))

    each(last + 1, ahead)

    def clear():
        dk_acc[...] = jnp.zeros(dk_acc.shape, f32)
        dv_acc[...] = jnp.zeros(dv_acc.shape, f32)

    def keep(c, halves=(0, 1)):
        for i in halves:
            at = slice(i * cells, (i + 1) * cells)
            cell_out[0, 2 * c + i] = dk_acc[at, :].astype(bf)
            cell_out[1, 2 * c + i] = dv_acc[at, :].astype(bf)

    def leave(c, halves=(0, 1)):
        keep(c, halves)
        for i in halves:
            grad_copy(0, dk_o, 2 * c + i).start()
            grad_copy(1, dv_o, 2 * c + i).start()

    clear()
    for i in range(2):
        half = parts[: len(parts) // 2] if i == 0 else parts[len(parts) // 2 :]
        each(dec, lambda t: backward(chunks - 1, t, half))
        leave(chunks - 1, (i,))

    def far_chunk(n):
        c = chunks - 2 - n
        clear()
        each(dec, lambda t: backward(c, t))
        leave(c)

    each(chunks - 3, far_chunk)

    def last_tokens(i):
        t = flip(spread, dec - 1 - i)
        backward_queries(t, 2)
        back_start(1, dq_out, dq_o, t)

    each(dec, last_tokens)
    clear()
    for n, acc, dst, step in ((1, dv_acc, dv_o, value_cells), (0, dk_acc, dk_o, key_cells)):
        each(dec, lambda t: step(1, t))
        for i in range(2):
            cell_out[n, 2 + i] = acc[i * cells : (i + 1) * cells, :].astype(bf)
            grad_copy(n, dst, 2 + i).start()
    clear()
    each(dec, lambda t: backward_cells(0, t))
    keep(0)
    for n, dst in ((0, dk_o), (1, dv_o)):
        grad_copy(n, dst, 1).start()
        grad_local(n, dst).start()

    token_sent(0)
    token_sent(1)
    for i in range(1, dec):
        bias_copy(i).wait_send()
    for d in range(1, enc):
        cell_copy(0, k, k_in, d).wait_send()
        cell_copy(1, v, v_in, d).wait_send()
    for n, dst in ((0, dk_o), (1, dv_o)):
        for d in range(1, enc):
            grad_copy(n, dst, d).wait_send()
            grad_wait(n, dst, d).wait_recv()
        grad_local(n, dst).wait()
    back_finish(0, ctx_out, ctx_o)
    back_finish(1, dq_out, dq_o)


def settle_kernel(*refs):
    src, dst, mid, sems = refs[:4], refs[4:8], refs[8:12], refs[12]
    steps = []
    for n, (a, m, b) in enumerate(zip(src, mid, dst)):
        for i in range(4):
            count = a.shape[0] // 4
            steps.append((
                pltpu.make_async_copy(rows_of(a, i, count), rows_of(m, i, count), sems.at[0, n, i]),
                pltpu.make_async_copy(rows_of(m, i, count), rows_of(b, i, count), sems.at[1, n, i]),
            ))
    for load, store in steps:
        load.start()
    for load, store in steps:
        load.wait()
        store.start()
    for load, store in steps:
        store.wait()


def settle(outs):
    return pl.pallas_call(
        settle_kernel,
        out_shape=[jax.ShapeDtypeStruct(x.shape, x.dtype) for x in outs],
        in_specs=[pl.BlockSpec(memory_space=pl.ANY)] * 4,
        out_specs=[pl.BlockSpec(memory_space=pl.ANY)] * 4,
        scratch_shapes=[pltpu.VMEM(x.shape, x.dtype) for x in outs]
        + [pltpu.SemaphoreType.DMA((2, 4, 4))],
        name="settle",
    )(*outs)


def fused(q, g, k, v, bias):
    enc, dec = lax.axis_size("enc"), lax.axis_size("dec")
    width = k.shape[1] // (enc * dec)
    heads = width // DH
    tok, chunk = q.shape[0], k.shape[0]
    bf, f32 = jnp.bfloat16, jnp.float32
    dma = pltpu.SemaphoreType.DMA
    vmem = pltpu.VMEM
    token_out = jax.ShapeDtypeStruct((tok, dec * width), bf)
    cell_out = jax.ShapeDtypeStruct((chunk, enc * width), bf)
    return pl.pallas_call(
        fused_kernel,
        out_shape=(token_out, token_out, cell_out, cell_out),
        in_specs=[pl.BlockSpec(memory_space=pl.ANY)] * 5,
        out_specs=[pl.BlockSpec(memory_space=pl.ANY)] * 4,
        scratch_shapes=[
            vmem((dec, tok, width), bf), vmem((dec, tok, width), bf),
            vmem((dec, tok, width), bf), vmem((dec, tok, width), bf),
            vmem((enc, chunk, width), bf), vmem((enc, chunk, width), bf),
            vmem((dec, bias.shape[0], tok), bf),
            vmem((enc // 2, heads, 2 * chunk, width), bf),
            vmem((enc // 2, heads, 2 * chunk, width), bf),
            vmem((enc // 2, width, 2 * chunk), bf),
            vmem((enc // 2, heads, DH + 16, 2 * chunk), bf),
            vmem((dec, heads, width, tok), bf), vmem((dec, width, tok), bf),
            vmem((heads, 2 * chunk, tok), f32), vmem((heads, 8, tok), f32),
            vmem((enc // 2, dec, heads, 2 * chunk, tok), bf),
            vmem((enc // 2, dec, heads, 8, tok), f32), vmem((dec, heads, 8, tok), f32),
            vmem((dec, heads, DH + 16, tok), f32),
            vmem((dec, heads, 8, tok), f32), vmem((dec, heads, 8, tok), f32),
            vmem((dec, width, tok), f32),
            vmem((2 * chunk, width), f32), vmem((2 * chunk, width), f32),
            vmem((2, enc, chunk, width), bf), vmem((dec, tok, width), bf),
            vmem((dec, tok, width), bf),
            dma((2, dec)), dma((2, dec)), dma((2, dec)), dma((2, dec)), dma((dec,)), dma((dec,)),
            dma((2, enc)), dma((2, enc)), dma((2, enc)), dma((2, enc)),
            dma((2, dec)), dma((2, dec)), dma((9,)),
        ],
        compiler_params=pltpu.CompilerParams(
            collective_id=0, has_side_effects=True, vmem_limit_bytes=60 * 1024 * 1024
        ),
        name="fused",
    )(q, g, k, v, bias)


def shared_head(q, g, k, v, bias, per, dec):
    share = DH // q.shape[1]
    mates = [
        [per * (j + i) + c for i in range(share)] for c in range(per) for j in range(0, dec, share)
    ]
    place = lax.rem(lax.axis_index("enc") // per, share)
    rows = q.shape[0] // share

    def to_head(x):
        return lax.all_to_all(x, "enc", 0, 1, axis_index_groups=mates, tiled=True)

    def from_head(x):
        return lax.all_to_all(x, "enc", 1, 0, axis_index_groups=mates, tiled=True)

    def widen(x):
        return lax.all_gather(x, "enc", axis=1, axis_index_groups=mates, tiled=True)

    def add_up(x):
        total = lax.psum_scatter(
            x, "enc", scatter_dimension=1, axis_index_groups=mates, tiled=True
        )
        return total.astype(jnp.bfloat16)

    bias = lax.dynamic_slice_in_dim(bias, place * rows, rows, 1)
    ctx, dq, dk, dv = attention(to_head(q), to_head(g), widen(k), widen(v), bias, jnp.float32)
    return from_head(ctx), from_head(dq), add_up(dk), add_up(dv)


def body(queries, out_grad, memory_keys, memory_values, ref_blocks, ref_counts):
    enc, dec = lax.axis_size("enc"), lax.axis_size("dec")
    per = enc // dec
    tok, tok_width = queries.shape
    own_cells, full = memory_keys.shape
    width = full // (enc * dec)
    groups = [[per * k + c for k in range(dec)] for c in range(per)]

    def token_in(x):
        x = x.reshape(tok, dec, width).transpose(1, 0, 2)
        x = lax.all_to_all(x, "enc", 0, 0, axis_index_groups=groups)
        return lax.all_to_all(x, "dec", 0, 0).reshape(dec * tok, width)

    def token_out(x):
        x = lax.all_to_all(x.reshape(dec, tok, width), "dec", 0, 0)
        x = lax.all_to_all(x, "enc", 0, 0, axis_index_groups=groups)
        return x.transpose(1, 0, 2).reshape(tok, tok_width)

    def cell_in(x):
        x = lax.dynamic_slice_in_dim(x, lax.axis_index("dec") * (full // dec), full // dec, 1)
        x = x.reshape(own_cells, per, dec, width).transpose(2, 1, 0, 3)
        x = lax.all_to_all(x.reshape(enc, own_cells, width), "enc", 0, 0)
        return x.reshape(enc * own_cells, width)

    def cell_out(x):
        x = lax.all_to_all(x.reshape(enc, own_cells, width), "enc", 0, 0)
        x = x.reshape(dec, per, own_cells, width).transpose(2, 1, 0, 3)
        return x.reshape(own_cells, full // dec)

    bias = hidden_blocks(ref_blocks, ref_counts, enc * own_cells // BLOCK)
    small = enc * own_cells // BLOCK <= DH
    if width == LANES and enc == 8 and dec == 4 and small:
        return tuple(settle(fused(queries, out_grad, memory_keys, memory_values, bias)))
    bias = lax.all_gather(bias, "dec", axis=1, tiled=True)
    q, g, k, v = token_in(queries), token_in(out_grad), cell_in(memory_keys), cell_in(memory_values)
    if width >= DH:
        ctx, dq, dk, dv = attention(q, g, k, v, bias)
    else:
        ctx, dq, dk, dv = shared_head(q, g, k, v, bias, per, dec)
    return token_out(ctx), token_out(dq), cell_out(dk), cell_out(dv)


def solution(mesh):
    in_specs = (
        P("dec", "enc"),
        P("dec", "enc"),
        P("enc", None),
        P("enc", None),
        P("dec", None),
        P("dec"),
    )
    out_specs = (P("dec", "enc"), P("dec", "enc"), P("enc", "dec"), P("enc", "dec"))
    return jax.shard_map(body, mesh=mesh, in_specs=in_specs, out_specs=out_specs, check_vma=False)
```
